32 devices in a mesh: dev: 32 (over z, y, x, core).
Axes of the slice: x: 2, y: 2, z: 4, core: 2. Of those that a mesh axis runs over, the one named last changes fastest.
Arguments:
- state: float32 [5, 64, 16384], P(None, None, 'dev'), as said below
- step_size: float32 [1], replicated, may hold values from 0.0003 to 0.0006
- levels: int32 [16384], P('dev'), may hold values from 6 to 7, as said below
- send_faces: int32 [256, 128], P('dev'), may hold values from 0 to 3072, as said below
- partner: int32 [6, 16384], P(None, 'dev'), may hold values from 0 to 4096, as said below
- mortar_in: int32 [5, 1280], P(None, 'dev'), may hold values from 0 to 4096, as said below
- mortar_dir: int32 [1280], P('dev'), may hold values from 0 to 3, as said below
- return_faces: int32 [64, 32], P('dev'), may hold values from 0 to 200, as said below
- flux_source: int32 [6, 16384], P(None, 'dev'), may hold values from 0 to 264, as said below
Outputs:
- increment: float32 [5, 64, 16384], P(None, None, 'dev')
The draws below stay inside these ranges and needn't reach their ends.
Inputs may be any that keep to these rules, and one draw needn't show every extreme that they name: At every node the entries are density, momenta and total energy of a state with density from 1 to 1.5, velocity components from -0.2 to 0.2 and pressure from 1 to 1.5. `levels`: every element has level 6 or 7. `send_faces`: row 8 d + p lists local face numbers of device d whose traces its peer p needs; 3072 marks an empty entry. Faces are either conforming (opposite faces of two elements of one level, each the other's partner) or hanging (one face and four faces of elements one level finer meet in exactly one mortar); partners lie within 4 devices along the curve, mortars join faces of one device or of two adjacent ones. Hanging faces have partner 6 * 512. `mortar_in`: unused mortar entries name 3072 in all five rows. `mortar_dir`: unused mortar entries have 0. `return_faces`: 200 marks an empty entry. `flux_source`: 200 exactly for conforming faces.
All inputs are finite; a program needn't handle non-finite values.
Results may differ from the reference program's by a relative error of at most 0.0003.
Values sent between devices are 32-bit elements; how exact they have to be, the bound alone decides.
No kernel may reach another device: no remote copies, remote signals or barrier semaphores. Data moves between devices by JAX's collectives and lax.ppermute only.
A program may use at most 64 MiB of HBM per device.

```python
import math
import jax
import jax.numpy as jnp
import numpy as np
from jax import lax

ELEM_DEV = 512
ELEMS = 16384
HOP = 4
PEERS = 8
SLOTS = 128
CROSS_HANG = 8
RETURN_SLOTS = 32
MORTAR_SLOTS = 40
LEVEL = 6
N_DEV = 32


def device_random(key, device):
    fine_least = ELEM_DEV // 128
    fine_most = 3 * ELEM_DEV // 64
    forced = jax.random.randint(jax.random.fold_in(key, 101), (2,), 0, N_DEV)
    own_key = jax.random.fold_in(jax.random.fold_in(key, 102), device)
    groups = jax.random.randint(jax.random.fold_in(own_key, 1), (), fine_least, fine_most + 1)
    groups = jnp.where(device == forced[1], fine_most, groups)
    ranking = jax.random.permutation(jax.random.fold_in(own_key, 2), ELEM_DEV // 8)
    fine = jnp.repeat((ranking < groups).astype(jnp.int32), 8)
    orders = []
    for face in range(6):
        shuffle = jax.random.permutation(jax.random.fold_in(own_key, 3 + face), ELEM_DEV)
        orders.append(jnp.argsort(fine * ELEM_DEV + shuffle, stable=True).astype(jnp.int32))
    places = [jax.random.permutation(jax.random.fold_in(own_key, 10 + peer), SLOTS).astype(jnp.int32) for peer in range(PEERS)]
    backs = [jax.random.permutation(jax.random.fold_in(own_key, 40 + side), RETURN_SLOTS).astype(jnp.int32) for side in range(2)]
    mortar_places = jax.random.permutation(jax.random.fold_in(own_key, 50), MORTAR_SLOTS).astype(jnp.int32)
    owner_bit = jax.random.randint(jax.random.fold_in(own_key, 51), (), 0, 2)
    owner_bit = jnp.where(device == forced[0], 1, jnp.where(device == (forced[0] + 1) % N_DEV, 0, owner_bit))
    return {'groups': groups, 'fine': fine, 'orders': orders, 'places': places, 'backs': backs, 'mortar_places': mortar_places, 'owner_bit': owner_bit}


def build_device(key, device):
    here = device_random(key, device)
    beside_all = {}
    for offset in range(1, HOP + 1):
        beside_all[offset] = device_random(key, (device + offset) % N_DEV)
        beside_all[-offset] = device_random(key, (device - offset) % N_DEV)
    width = ELEM_DEV
    empty_trace = 6 * width
    base = empty_trace + 1
    empty_flux = 5 * MORTAR_SLOTS
    return_base = empty_flux + 1
    hang = CROSS_HANG
    first_cut = SLOTS - 4 * hang
    big_start = first_cut + SLOTS
    coarse_count = width - 8 * here['groups']
    local_pairs = here['groups'] // 2
    bit_here = here['owner_bit']
    bit_before = beside_all[-1]['owner_bit']
    orders = here['orders']

    def take(table, index, limit):
        return table[jnp.clip(index, 0, limit - 1)]

    def received(peer_offset, index):
        peer = peer_offset - 1 if peer_offset > 0 else HOP - peer_offset - 1
        return base + peer * SLOTS + take(beside_all[-peer_offset]['places'][peer], index, SLOTS)

    def returned(side, index):
        sender = beside_all[-1] if side == 0 else beside_all[1]
        return return_base + side * RETURN_SLOTS + take(sender['backs'][side], index, RETURN_SLOTS)

    def mortar_slot(index):
        return take(here['mortar_places'], index, MORTAR_SLOTS)
    rank = jnp.arange(width, dtype=jnp.int32)
    fine_rank = rank - coarse_count
    fine_pos = jnp.clip(fine_rank, 0, width - 1)
    defaults = [(face ^ 1) * width + orders[face ^ 1][rank] for face in range(6)]
    coarse_hang = rank < local_pairs
    fine_hang = (fine_rank >= 0) & (fine_rank < 4 * local_pairs)
    quarter_flux = (1 + fine_pos % 4) * MORTAR_SLOTS
    partner_zero = jnp.where(coarse_hang | fine_hang, empty_trace, defaults[0])
    flux_zero = jnp.where(coarse_hang, mortar_slot(local_pairs + rank), jnp.where(fine_hang, quarter_flux + mortar_slot(fine_pos // 4), empty_flux))
    partner_one = jnp.where(coarse_hang | fine_hang, empty_trace, defaults[1])
    flux_one = jnp.where(coarse_hang, mortar_slot(rank), jnp.where(fine_hang, quarter_flux + mortar_slot(local_pairs + fine_pos // 4), empty_flux))
    nearest = rank < first_cut
    second = (rank >= first_cut) & (rank < big_start)
    bigs = (rank >= big_start) & (rank < big_start + hang)
    smalls = (fine_rank >= 0) & (fine_rank < 4 * hang)
    big_index = rank - big_start
    partner_two = jnp.where(nearest, received(1, rank), jnp.where(second, received(2, rank - first_cut), jnp.where(bigs | smalls, empty_trace, defaults[2])))
    flux_two = jnp.where(bigs, jnp.where(bit_before == 1, mortar_slot(2 * local_pairs + hang + big_index), returned(0, big_index)), jnp.where(smalls, jnp.where(bit_before == 1, returned(0, fine_pos), quarter_flux + mortar_slot(2 * local_pairs + hang + fine_pos // 4)), empty_flux))
    partner_three = jnp.where(nearest, received(-1, rank), jnp.where(second, received(-2, rank - first_cut), jnp.where(bigs | smalls, empty_trace, defaults[3])))
    flux_three = jnp.where(bigs, jnp.where(bit_here == 1, mortar_slot(2 * local_pairs + big_index), returned(1, big_index)), jnp.where(smalls, jnp.where(bit_here == 1, returned(1, fine_pos), quarter_flux + mortar_slot(2 * local_pairs + fine_pos // 4)), empty_flux))
    partner_four = jnp.where(rank < SLOTS, received(3, rank), jnp.where(rank < 2 * SLOTS, received(4, rank - SLOTS), defaults[4]))
    partner_five = jnp.where(rank < SLOTS, received(-3, rank), jnp.where(rank < 2 * SLOTS, received(-4, rank - SLOTS), defaults[5]))
    conform_flux = jnp.full((width,), empty_flux, jnp.int32)
    by_rank = [partner_zero, partner_one, partner_two, partner_three, partner_four, partner_five]
    flux_rank = [flux_zero, flux_one, flux_two, flux_three, conform_flux, conform_flux]
    partner = jnp.stack([jnp.zeros((width,), jnp.int32).at[orders[face]].set(by_rank[face].astype(jnp.int32)) for face in range(6)])
    sources = jnp.stack([jnp.zeros((width,), jnp.int32).at[orders[face]].set(flux_rank[face].astype(jnp.int32)) for face in range(6)])
    slot = jnp.arange(SLOTS, dtype=jnp.int32)
    extra = slot - first_cut
    plus_y = orders[3]
    minus_y = orders[2]
    forward_one = jnp.where(slot < first_cut, 3 * width + take(plus_y, slot, width), jnp.where(bit_here == 1, jnp.where(extra < 4 * hang, 3 * width + take(plus_y, coarse_count + extra, width), empty_trace), jnp.where(extra < hang, 3 * width + take(plus_y, big_start + extra, width), empty_trace)))
    backward_one = jnp.where(slot < first_cut, 2 * width + take(minus_y, slot, width), jnp.where(bit_before == 1, jnp.where(extra < 4 * hang, 2 * width + take(minus_y, coarse_count + extra, width), empty_trace), jnp.where(extra < hang, 2 * width + take(minus_y, big_start + extra, width), empty_trace)))
    lists = [forward_one, 3 * width + take(plus_y, first_cut + slot, width), 5 * width + take(orders[5], slot, width), 5 * width + take(orders[5], SLOTS + slot, width), backward_one, 2 * width + take(minus_y, first_cut + slot, width), 4 * width + take(orders[4], slot, width), 4 * width + take(orders[4], SLOTS + slot, width)]
    sends = jnp.stack([jnp.full((SLOTS,), empty_trace, jnp.int32).at[here['places'][peer]].set(lists[peer].astype(jnp.int32)) for peer in range(PEERS)])
    entry = jnp.arange(MORTAR_SLOTS, dtype=jnp.int32)
    in_local_a = entry < local_pairs
    in_local_b = (entry >= local_pairs) & (entry < 2 * local_pairs)
    in_after = (entry >= 2 * local_pairs) & (entry < 2 * local_pairs + hang)
    in_before = (entry >= 2 * local_pairs + hang) & (entry < 2 * local_pairs + 2 * hang)
    index_b = entry - local_pairs
    index_after = entry - 2 * local_pairs
    index_before = entry - 2 * local_pairs - hang
    big = jnp.where(in_local_a, width + take(orders[1], entry, width), jnp.where(in_local_b, take(orders[0], index_b, width), jnp.where(in_after, jnp.where(bit_here == 1, 3 * width + take(plus_y, big_start + index_after, width), received(-1, first_cut + index_after)), jnp.where(in_before, jnp.where(bit_before == 1, 2 * width + take(minus_y, big_start + index_before, width), received(1, first_cut + index_before)), empty_trace))))

    def small(quarter):
        return jnp.where(in_local_a, take(orders[0], coarse_count + 4 * entry + quarter, width), jnp.where(in_local_b, width + take(orders[1], coarse_count + 4 * index_b + quarter, width), jnp.where(in_after, jnp.where(bit_here == 1, received(-1, first_cut + 4 * index_after + quarter), 3 * width + take(plus_y, coarse_count + 4 * index_after + quarter, width)), jnp.where(in_before, jnp.where(bit_before == 1, received(1, first_cut + 4 * index_before + quarter), 2 * width + take(minus_y, coarse_count + 4 * index_before + quarter, width)), empty_trace))))
    direction = jnp.where(in_local_a, 1, jnp.where(in_local_b, 0, jnp.where(in_after, jnp.where(bit_here == 1, 3, 2), jnp.where(in_before, jnp.where(bit_before == 1, 2, 3), 0))))
    entries = jnp.stack([big] + [small(quarter) for quarter in range(4)]).astype(jnp.int32)
    mortar_in = jnp.zeros((5, MORTAR_SLOTS), jnp.int32).at[:, here['mortar_places']].set(entries)
    mortar_dir = jnp.zeros((MORTAR_SLOTS,), jnp.int32).at[here['mortar_places']].set(direction.astype(jnp.int32))
    back_slot = jnp.arange(RETURN_SLOTS, dtype=jnp.int32)
    quarter_of = (1 + back_slot % 4) * MORTAR_SLOTS
    pair_of = back_slot // 4
    to_after = jnp.where(bit_here == 1, quarter_of + mortar_slot(2 * local_pairs + pair_of), jnp.where(back_slot < hang, mortar_slot(2 * local_pairs + back_slot), empty_flux))
    to_before = jnp.where(bit_before == 1, quarter_of + mortar_slot(2 * local_pairs + hang + pair_of), jnp.where(back_slot < hang, mortar_slot(2 * local_pairs + hang + back_slot), empty_flux))
    back_lists = [to_after, to_before]
    returns = jnp.stack([jnp.full((RETURN_SLOTS,), empty_flux, jnp.int32).at[here['backs'][side]].set(back_lists[side].astype(jnp.int32)) for side in range(2)])
    levels = (LEVEL + here['fine']).astype(jnp.int32)
    return (levels, sends, partner, mortar_in, mortar_dir, returns, sources)


def mesh_part(key, which):
    devices = jnp.arange(N_DEV, dtype=jnp.int32)
    built = jax.vmap(build_device, in_axes=(None, 0))(jax.random.fold_in(key, 7), devices)
    return built[which]


def draw_levels(key, part):
    return mesh_part(key, 0).reshape(ELEMS)


def draw_send_faces(key, part):
    return mesh_part(key, 1).reshape(N_DEV * PEERS, SLOTS)


def draw_partner(key, part):
    return jnp.transpose(mesh_part(key, 2), (1, 0, 2)).reshape(6, ELEMS)


def draw_mortar_in(key, part):
    return jnp.transpose(mesh_part(key, 3), (1, 0, 2)).reshape(5, N_DEV * MORTAR_SLOTS)


def draw_mortar_dir(key, part):
    return mesh_part(key, 4).reshape(N_DEV * MORTAR_SLOTS)


def draw_return_faces(key, part):
    return mesh_part(key, 5).reshape(2 * N_DEV, RETURN_SLOTS)


def draw_flux_source(key, part):
    return jnp.transpose(mesh_part(key, 6), (1, 0, 2)).reshape(6, ELEMS)


def draw_state(key, part):
    keys = jax.random.split(key, 3)
    shape = (64, ELEMS)
    density = jax.random.uniform(keys[0], shape, minval=1.0, maxval=1.5)
    motion = jax.random.uniform(keys[1], (3,) + shape, minval=-0.2, maxval=0.2)
    pressure = jax.random.uniform(keys[2], shape, minval=1.0, maxval=1.5)
    energy = pressure / 0.4 + 0.5 * density * (motion[0] * motion[0] + motion[1] * motion[1] + motion[2] * motion[2])
    return jnp.stack([density, density * motion[0], density * motion[1], density * motion[2], energy]).astype(jnp.float32)


def level_of(stream_key, dims, cuts, least, largest):
    loudness = 1.0
    for axis_at, blocks in cuts:
        steps = jax.random.uniform(jax.random.fold_in(jax.random.fold_in(stream_key, 6), axis_at), (blocks,), jnp.float32, least / len(cuts), largest / len(cuts))
        loudness = loudness * jnp.repeat(jnp.exp(steps), dims[axis_at] // blocks).reshape((-1,) + (1,) * (len(dims) - 1 - axis_at))
    return loudness


def setup_inputs(seed: int = 0) -> dict:
    key_of = jax.random.split(jax.random.key(seed), 10)
    return {
        "state": draw_state(jax.random.fold_in(key_of[9], 71), 0),
        "step_size": jnp.clip(jnp.exp(jax.random.uniform(key_of[1], (1,), jnp.float32, math.log(0.0003), math.log(0.0006))), 0.0003, 0.0006),
        "levels": draw_levels(jax.random.fold_in(key_of[9], 71), 0),
        "send_faces": draw_send_faces(jax.random.fold_in(key_of[9], 71), 0),
        "partner": draw_partner(jax.random.fold_in(key_of[9], 71), 0),
        "mortar_in": draw_mortar_in(jax.random.fold_in(key_of[9], 71), 0),
        "mortar_dir": draw_mortar_dir(jax.random.fold_in(key_of[9], 71), 0),
        "return_faces": draw_return_faces(jax.random.fold_in(key_of[9], 71), 0),
        "flux_source": draw_flux_source(jax.random.fold_in(key_of[9], 71), 0),
    }


GAMMA = 1.4
HIGHEST = lax.Precision.HIGHEST

def lobatto_tables():
    nodes = np.array([-1.0, -1.0 / np.sqrt(5.0), 1.0 / np.sqrt(5.0), 1.0])
    weights = np.array([1.0, 5.0, 5.0, 1.0]) / 6.0

    def basis(points):
        table = np.ones((len(points), 4))
        for column in range(4):
            for other in range(4):
                if other != column:
                    table[:, column] *= (points - nodes[other]) / (nodes[column] - nodes[other])
        return table
    derivative = np.zeros((4, 4))
    for row in range(4):
        for column in range(4):
            total = 0.0
            for other in range(4):
                if other != column:
                    term = 1.0 / (nodes[column] - nodes[other])
                    for third in range(4):
                        if third != column and third != other:
                            term *= (nodes[row] - nodes[third]) / (nodes[column] - nodes[third])
                    total += term
            derivative[row, column] = total
    lower = basis((nodes - 1.0) / 2.0)
    upper = basis((nodes + 1.0) / 2.0)
    back_lower = 0.5 * (lower.T * weights[None, :]) / weights[:, None]
    back_upper = 0.5 * (upper.T * weights[None, :]) / weights[:, None]
    return [np.asarray(table, np.float32) for table in (derivative, lower, upper, back_lower, back_upper)]

def face_node_table():
    table = np.zeros((6, 16), np.int32)
    for face in range(6):
        axis = face // 2
        others = [dimension for dimension in range(3) if dimension != axis]
        count = 0
        for first in range(4):
            for second in range(4):
                spot = [0, 0, 0]
                spot[axis] = 3 * (face % 2)
                spot[others[0]] = first
                spot[others[1]] = second
                table[face, count] = 16 * spot[0] + 4 * spot[1] + spot[2]
                count += 1
    return table

def face_normals(count):
    signs = np.zeros((3, 6), np.float32)
    for face in range(6):
        signs[face // 2, face] = 2.0 * (face % 2) - 1.0
    return tuple((jnp.asarray(np.repeat(signs[axis], count)) for axis in range(3)))

def reference_state(count):
    values = jnp.array([1.0, 0.0, 0.0, 0.0, 2.5], jnp.float32)
    return jnp.broadcast_to(values[:, None, None], (5, 16, count))

def normal_flux(state, normal):
    density = state[0]
    motion = [state[1 + axis] / density for axis in range(3)]
    pressure = (GAMMA - 1.0) * (state[4] - 0.5 * (state[1] * motion[0] + state[2] * motion[1] + state[3] * motion[2]))
    along = motion[0] * normal[0] + motion[1] * normal[1] + motion[2] * normal[2]
    flux = jnp.stack([state[0] * along, state[1] * along + pressure * normal[0], state[2] * along + pressure * normal[1], state[3] * along + pressure * normal[2], (state[4] + pressure) * along])
    speed = jnp.abs(along) + jnp.sqrt(GAMMA * pressure / density)
    return (flux, speed)

def rusanov(inside, inside_flux, inside_speed, outside, normal):
    outside_flux, outside_speed = normal_flux(outside, normal)
    return 0.5 * (inside_flux + outside_flux) - 0.5 * jnp.maximum(inside_speed, outside_speed) * (outside - inside)

def face_traces(block):
    cube = block.reshape(5, 4, 4, 4, block.shape[-1])
    faces = [cube[:, 0], cube[:, 3], cube[:, :, 0], cube[:, :, 3], cube[:, :, :, 0], cube[:, :, :, 3]]
    return jnp.concatenate([face.reshape(5, 16, block.shape[-1]) for face in faces], axis=2)

def volume_term(block, scale):
    cube = block.reshape(5, 4, 4, 4, block.shape[-1])
    derivative = jnp.asarray(lobatto_tables()[0])
    first, _ = normal_flux(cube, (1.0, 0.0, 0.0))
    second, _ = normal_flux(cube, (0.0, 1.0, 0.0))
    third, _ = normal_flux(cube, (0.0, 0.0, 1.0))
    total = jnp.einsum('ai,vijke->vajke', derivative, first, precision=HIGHEST)
    total = total + jnp.einsum('bj,vijke->vibke', derivative, second, precision=HIGHEST)
    total = total + jnp.einsum('ck,vijke->vijce', derivative, third, precision=HIGHEST)
    return -scale * total

def add_lift(residual, jump, scale):
    count = residual.shape[-1]
    parts = -6.0 * scale * jump.reshape(5, 4, 4, 6, count)
    residual = residual.at[:, 0].add(parts[:, :, :, 0])
    residual = residual.at[:, 3].add(parts[:, :, :, 1])
    residual = residual.at[:, :, 0].add(parts[:, :, :, 2])
    residual = residual.at[:, :, 3].add(parts[:, :, :, 3])
    residual = residual.at[:, :, :, 0].add(parts[:, :, :, 4])
    residual = residual.at[:, :, :, 3].add(parts[:, :, :, 5])
    return residual

def mortar_fluxes(big, smalls, direction):
    tables = lobatto_tables()
    forward = (jnp.asarray(tables[1]), jnp.asarray(tables[2]))
    backward = (jnp.asarray(tables[3]), jnp.asarray(tables[4]))
    count = big.shape[-1]
    normal = tuple(((direction == 2 * axis + 1).astype(jnp.float32) - (direction == 2 * axis).astype(jnp.float32) for axis in range(3)))
    square = big.reshape(5, 4, 4, count)
    gathered = jnp.zeros_like(big)
    pieces = []
    for quarter in range(4):
        near = jnp.einsum('ai,bj,vijm->vabm', forward[quarter % 2], forward[quarter // 2], square, precision=HIGHEST).reshape(5, 16, count)
        near_flux, near_speed = normal_flux(near, normal)
        star = rusanov(near, near_flux, near_speed, smalls[quarter], normal)
        pieces.append(-star)
        gathered = gathered + jnp.einsum('ai,bj,vijm->vabm', backward[quarter % 2], backward[quarter // 2], star.reshape(5, 4, 4, count), precision=HIGHEST).reshape(5, 16, count)
    return jnp.concatenate([gathered] + pieces, axis=2)

def reference(state, step_size, levels, send_faces, partner, mortar_in, mortar_dir, return_faces, flux_source):
    offsets = jnp.concatenate([jnp.arange(1, HOP + 1, dtype=jnp.int32), -jnp.arange(1, HOP + 1, dtype=jnp.int32)]).astype(jnp.int32)
    nodes = jnp.asarray(face_node_table())
    empty_trace = 6 * ELEM_DEV
    empty_flux = 5 * MORTAR_SLOTS
    all_slots = N_DEV * MORTAR_SLOTS

    def global_trace(local, device):
        own = local // ELEM_DEV * ELEMS + device * ELEM_DEV + local % ELEM_DEV
        beyond = jnp.clip(local - empty_trace - 1, 0, PEERS * SLOTS - 1)
        peer = beyond // SLOTS
        sender = (device - offsets[peer]) % N_DEV
        sent = jnp.clip(send_faces[sender * PEERS + peer, beyond % SLOTS], 0, empty_trace - 1)
        remote = sent // ELEM_DEV * ELEMS + sender * ELEM_DEV + sent % ELEM_DEV
        return jnp.where(local < empty_trace, own, jnp.where(local == empty_trace, 6 * ELEMS, remote)).astype(jnp.int32)

    def fetch(index):
        flat = index.reshape(-1)
        face = jnp.clip(flat // ELEMS, 0, 5)
        element = flat % ELEMS
        values = jnp.transpose(state[:, nodes[face], element[:, None]], (0, 2, 1))
        return jnp.where((flat == 6 * ELEMS)[None, None, :], reference_state(flat.shape[0]), values)

    def global_flux(local, device):
        own = local // MORTAR_SLOTS * all_slots + device * MORTAR_SLOTS + local % MORTAR_SLOTS
        beyond = jnp.clip(local - empty_flux - 1, 0, 2 * RETURN_SLOTS - 1)
        side = beyond // RETURN_SLOTS
        sender = (device - 1 + 2 * side) % N_DEV
        sent = jnp.clip(return_faces[sender * 2 + side, beyond % RETURN_SLOTS], 0, empty_flux - 1)
        remote = sent // MORTAR_SLOTS * all_slots + sender * MORTAR_SLOTS + sent % MORTAR_SLOTS
        return jnp.where(local < empty_flux, own, jnp.where(local == empty_flux, 5 * all_slots, remote)).astype(jnp.int32)
    slot_device = jnp.arange(all_slots, dtype=jnp.int32) // MORTAR_SLOTS
    sources = [fetch(global_trace(mortar_in[row], slot_device)) for row in range(5)]
    mortars = mortar_fluxes(sources[0], sources[1:], mortar_dir)
    mortars = jnp.concatenate([mortars, jnp.zeros((5, 16, 1), jnp.float32)], axis=2)
    normals = face_normals(ELEM_DEV)

    def one_device(device):
        block = lax.dynamic_slice_in_dim(state, device * ELEM_DEV, ELEM_DEV, 2)
        scale = jnp.exp2(lax.dynamic_slice_in_dim(levels, device * ELEM_DEV, ELEM_DEV, 0).astype(jnp.float32) + 1.0)
        local = face_traces(block)
        local_flux, local_speed = normal_flux(local, normals)
        links = lax.dynamic_slice_in_dim(partner, device * ELEM_DEV, ELEM_DEV, 1).reshape(-1)
        outside = fetch(global_trace(links, device))
        conforming = rusanov(local, local_flux, local_speed, outside, normals)
        anchors = lax.dynamic_slice_in_dim(flux_source, device * ELEM_DEV, ELEM_DEV, 1).reshape(-1)
        from_mortar = mortars[:, :, global_flux(anchors, device)]
        star = jnp.where((anchors != empty_flux)[None, None, :], from_mortar, conforming)
        residual = add_lift(volume_term(block, scale), star - local_flux, scale)
        return step_size[0] * residual.reshape(5, 64, ELEM_DEV)
    blocks = lax.map(one_device, jnp.arange(N_DEV, dtype=jnp.int32))
    return jnp.transpose(blocks, (1, 2, 0, 3)).reshape(5, 64, ELEMS)
```

```python
import functools

import jax
import jax.numpy as jnp
import numpy as np
from jax import lax
from jax.experimental import pallas as pl
from jax.experimental.pallas import tpu as pltpu
from jax.sharding import PartitionSpec as P

GAMMA = 1.4
HIGHEST = lax.Precision.HIGHEST
F32 = jnp.float32
BF16 = jnp.bfloat16
LANES = 128


def passed_along(block, axis, distance):
    devices = range(lax.axis_size(axis))
    route = [((i - distance) % len(devices), i) for i in devices]
    return lax.ppermute(block, axis, route)


def lobatto_tables():
    nodes = np.array([-1.0, -1.0 / np.sqrt(5.0), 1.0 / np.sqrt(5.0), 1.0])
    weights = np.array([1.0, 5.0, 5.0, 1.0]) / 6.0

    def basis(points):
        table = np.ones((len(points), 4))
        for column in range(4):
            for other in range(4):
                if other != column:
                    table[:, column] *= (points - nodes[other]) / (nodes[column] - nodes[other])
        return table

    derivative = np.zeros((4, 4))
    for row in range(4):
        for column in range(4):
            total = 0.0
            for other in range(4):
                if other != column:
                    term = 1.0 / (nodes[column] - nodes[other])
                    for third in range(4):
                        if third != column and third != other:
                            term *= (nodes[row] - nodes[third]) / (nodes[column] - nodes[third])
                    total += term
            derivative[row, column] = total
    lower = basis((nodes - 1.0) / 2.0)
    upper = basis((nodes + 1.0) / 2.0)
    back_lower = 0.5 * (lower.T * weights[None, :]) / weights[:, None]
    back_upper = 0.5 * (upper.T * weights[None, :]) / weights[:, None]
    return [
        np.asarray(table, np.float32)
        for table in (derivative, lower, upper, back_lower, back_upper)
    ]


def operator_tables():
    derivative, lower, upper, back_lower, back_upper = lobatto_tables()
    eye = np.eye(4, dtype=np.float32)
    volume = np.concatenate(
        [
            np.kron(derivative, np.kron(eye, eye)),
            np.kron(eye, np.kron(derivative, eye)),
            np.kron(eye, np.kron(eye, derivative)),
        ],
        axis=1,
    )
    five = np.eye(5, dtype=np.float32)
    forward, backward = (lower, upper), (back_lower, back_upper)
    spread = np.concatenate(
        [np.kron(five, np.kron(forward[q % 2], forward[q // 2])) for q in range(4)], axis=0
    )
    gather = np.concatenate(
        [np.kron(five, np.kron(backward[q % 2], backward[q // 2])) for q in range(4)], axis=1
    )
    return volume, spread, gather


def face_rows(ref, lanes, var, face):
    if face == 0:
        return ref[var, 0:16, :]
    if face == 1:
        return ref[var, 48:64, :]
    if face < 4:
        start = 12 * (face % 2)
        return jnp.concatenate(
            [ref[var, 16 * i + start : 16 * i + start + 4, :] for i in range(4)], axis=0
        )
    return jnp.concatenate(
        [
            lanes[block, pl.ds(64 * var + 3 * (face % 2), 16, stride=4), :]
            for block in range(lanes.shape[0])
        ],
        axis=1,
    )


def by_lanes(ref, lanes):
    for block in range(lanes.shape[0]):
        for var in range(5):
            lanes[block, 64 * var : 64 * var + 64, :] = ref[
                var, :, block * LANES : (block + 1) * LANES
            ]


def add_face(lanes, var, face, value):
    base = 64 * var
    for block in range(lanes.shape[0]):
        part = value[:, block * LANES : (block + 1) * LANES]
        if face < 2:
            lanes[block, base + 48 * face : base + 48 * face + 16, :] += part
        elif face < 4:
            start = base + 12 * (face % 2)
            for i in range(4):
                lanes[block, start + 16 * i : start + 16 * i + 4, :] += part[4 * i : 4 * i + 4]
        else:
            lanes[block, pl.ds(base + 3 * (face % 2), 16, stride=4), :] += part


def from_lanes(lanes, ref):
    for block in range(lanes.shape[0]):
        for var in range(5):
            ref[var, :, block * LANES : (block + 1) * LANES] = lanes[
                block, 64 * var : 64 * var + 64, :
            ]


def three_pieces(value):
    high = value.astype(BF16)
    rest = value - high.astype(F32)
    middle = rest.astype(BF16)
    low = (rest - middle.astype(F32)).astype(BF16)
    return high, middle, low


def store_pieces(pieces, rows, columns, value):
    for which, piece in enumerate(three_pieces(value)):
        pieces[80 * which + rows : 80 * which + rows + value.shape[0], columns] = piece


def one_hot(indices, count):
    spots = lax.broadcasted_iota(jnp.int32, (count, indices.shape[1]), 0)
    return (spots == indices).astype(F32).astype(BF16)


def joined(product):
    return (product[0:80] + product[80:160]) + product[160:240]


def primitives(cons):
    inverse = 1.0 / cons[0]
    motion = [cons[1 + axis] * inverse for axis in range(3)]
    pressure = (GAMMA - 1.0) * (
        cons[4] - 0.5 * (cons[1] * motion[0] + cons[2] * motion[1] + cons[3] * motion[2])
    )
    return inverse, motion, pressure


def axis_flux(cons, prim, axis, sign):
    _, motion, pressure = prim
    along = motion[axis] if sign > 0 else -motion[axis]
    push = pressure if sign > 0 else -pressure
    flux = [cons[v] * along for v in range(4)]
    flux[1 + axis] = flux[1 + axis] + push
    flux.append((cons[4] + pressure) * along)
    return flux


def sound(prim):
    inverse, _, pressure = prim
    return jnp.sqrt(GAMMA * pressure * inverse)


def normal_flux(cons, normal):
    inverse, motion, pressure = primitives(cons)
    along = motion[0] * normal[0] + motion[1] * normal[1] + motion[2] * normal[2]
    flux = [
        cons[0] * along,
        cons[1] * along + pressure * normal[0],
        cons[2] * along + pressure * normal[1],
        cons[3] * along + pressure * normal[2],
        (cons[4] + pressure) * along,
    ]
    return flux, jnp.abs(along) + jnp.sqrt(GAMMA * pressure * inverse)


def all_pieces(state_ref, lanes, pieces):
    elems = state_ref.shape[2]
    by_lanes(state_ref, lanes)
    for face in range(6):
        for var in range(5):
            store_pieces(
                pieces, 16 * var, slice(face * elems, (face + 1) * elems), face_rows(state_ref, lanes, var, face)
            )


def send_kernel(state_ref, faces_ref, *rest):
    outs, pieces, lanes = rest[:-2], rest[-2], rest[-1]
    elems = state_ref.shape[2]
    all_pieces(state_ref, lanes, pieces)
    slots = faces_ref.shape[1]
    for pair in range(len(outs) // 2):
        wanted = jnp.concatenate(
            [faces_ref[2 * pair : 2 * pair + 1, :], faces_ref[2 * pair + 1 : 2 * pair + 2, :]], axis=1
        )
        total = jnp.zeros((240, 2 * slots), F32)
        for face in range(6):
            total = total + jnp.dot(
                pieces[:, face * elems : (face + 1) * elems],
                one_hot(wanted - face * elems, elems),
                preferred_element_type=F32,
            )
        whole = joined(total)
        outs[2 * pair][...] = whole[:, :slots]
        outs[2 * pair + 1][...] = whole[:, slots:]


def local_kernel(
    state_ref, partner_ref, mortar_ref, factor_ref, volume_ref, acc_ref, beside_ref, big_ref, pieces, lanes, spots
):
    elems = state_ref.shape[2]
    all_pieces(state_ref, lanes, pieces)
    for face in range(6):
        product = jnp.dot(
            pieces[:, (face ^ 1) * elems : ((face ^ 1) + 1) * elems],
            one_hot(partner_ref[face : face + 1, :] - (face ^ 1) * elems, elems),
            preferred_element_type=F32,
        )
        beside_ref[:, face * elems : (face + 1) * elems] = joined(product)
    spots[...] = jnp.full(spots.shape, 6 * elems, jnp.int32)
    spots[0:5, 0 : mortar_ref.shape[1]] = mortar_ref[...]
    for row in range(5):
        wanted = spots[row : row + 1, :]
        total = jnp.zeros((240, LANES), F32)
        for face in range(6):
            total = total + jnp.dot(
                pieces[:, face * elems : (face + 1) * elems],
                one_hot(wanted - face * elems, elems),
                preferred_element_type=F32,
            )
        whole = joined(total)
        empty = wanted == 6 * elems
        for var, base in ((0, 1.0), (4, 2.5)):
            big_ref[16 * var : 16 * var + 16, row * LANES : (row + 1) * LANES] = jnp.where(
                empty, base, whole[16 * var : 16 * var + 16]
            )
        big_ref[16:64, row * LANES : (row + 1) * LANES] = whole[16:64]
    factor = factor_ref[...]
    cons = [state_ref[v] for v in range(5)]
    prim = primitives(cons)
    fluxes = [axis_flux(cons, prim, axis, 1) for axis in range(3)]
    for var in range(5):
        stacked = jnp.concatenate([fluxes[axis][var] for axis in range(3)], axis=0)
        acc_ref[var] = -factor * jnp.dot(
            volume_ref[...], stacked, preferred_element_type=F32, precision=HIGHEST
        )


def arrived_pieces(arrived, pieces):
    slots = arrived[0].shape[1]
    for peer, ref in enumerate(arrived):
        for var in range(5):
            store_pieces(
                pieces, 16 * var, slice(peer * slots, (peer + 1) * slots), ref[16 * var : 16 * var + 16, :]
            )


def mortar_kernel(base, *rest):
    arrived = rest[:8]
    big_ref, mortar_ref, way_ref, back_ref, spread_ref, gather_ref = rest[8:14]
    table_ref, leave_ref, next_ref, pieces, spots = rest[14:]
    count = mortar_ref.shape[1]
    arrived_pieces(arrived, pieces)
    spots[...] = jnp.full(spots.shape, base - 1, jnp.int32)
    spots[0:5, 0:count] = mortar_ref[...]
    spots[5:6, 0:count] = way_ref[...]
    traces = []
    for row in range(5):
        wanted = spots[row : row + 1, :] - base
        total = jnp.dot(pieces[...], one_hot(wanted, pieces.shape[1]), preferred_element_type=F32)
        traces.append(joined(total) + big_ref[:, row * LANES : (row + 1) * LANES])
    way = spots[5:6, :]
    normal = [
        (way == 2 * axis + 1).astype(F32) - (way == 2 * axis).astype(F32) for axis in range(3)
    ]
    near = jnp.dot(spread_ref[...], traces[0], preferred_element_type=F32, precision=HIGHEST)
    stars = []
    for quarter in range(4):
        first = [near[80 * quarter + 16 * v : 80 * quarter + 16 * v + 16] for v in range(5)]
        second = [traces[1 + quarter][16 * v : 16 * v + 16] for v in range(5)]
        first_flux, first_speed = normal_flux(first, normal)
        second_flux, second_speed = normal_flux(second, normal)
        speed = jnp.maximum(first_speed, second_speed)
        stars.append(
            jnp.concatenate(
                [
                    0.5 * (first_flux[v] + second_flux[v]) - 0.5 * speed * (second[v] - first[v])
                    for v in range(5)
                ],
                axis=0,
            )
        )
    stacked = jnp.concatenate(stars, axis=0)
    whole = jnp.dot(gather_ref[...], stacked, preferred_element_type=F32, precision=HIGHEST)
    valid = lax.broadcasted_iota(jnp.int32, (1, LANES), 1) < count
    table_ref[:, 0:LANES] = jnp.where(valid, whole, 0.0)
    for quarter in range(4):
        table_ref[:, (1 + quarter) * LANES : (2 + quarter) * LANES] = jnp.where(
            valid, -stars[quarter], 0.0
        )
    columns = table_ref.shape[1]
    for var in range(5):
        store_pieces(pieces, 16 * var, slice(0, columns), table_ref[16 * var : 16 * var + 16, :])
    spots[...] = jnp.full(spots.shape, 5 * count, jnp.int32)
    spots[0:2, 0 : back_ref.shape[1]] = back_ref[...]
    for side, out in enumerate((leave_ref, next_ref)):
        wanted = table_column(spots[side : side + 1, :], count)
        out[...] = joined(
            jnp.dot(pieces[:, 0:columns], one_hot(wanted, columns), preferred_element_type=F32)
        )


def table_column(entry, count):
    kind = sum((entry >= (k + 1) * count).astype(jnp.int32) for k in range(4))
    column = entry + kind * (LANES - count)
    return jnp.where(entry < 5 * count, column, -1)


def conform_kernel(
    base, state_ref, partner_ref, factor_ref, acc_ref, beside_ref, *rest
):
    arrived, out_ref, pieces, lanes, sums = rest[:8], rest[8], rest[9], rest[10], rest[11]
    elems = state_ref.shape[2]
    arrived_pieces(arrived, pieces)
    by_lanes(state_ref, lanes)
    by_lanes(acc_ref, sums)
    factor = -6.0 * factor_ref[...]
    for face in range(6):
        axis, sign = face // 2, 2 * (face % 2) - 1
        link = partner_ref[face : face + 1, :]
        product = jnp.dot(
            pieces[...], one_hot(link - base, pieces.shape[1]), preferred_element_type=F32
        )
        outside = joined(product) + beside_ref[:, face * elems : (face + 1) * elems]
        second = [outside[16 * v : 16 * v + 16] for v in range(5)]
        first = [face_rows(state_ref, lanes, v, face) for v in range(5)]
        first_prim, second_prim = primitives(first), primitives(second)
        first_flux = axis_flux(first, first_prim, axis, sign)
        second_flux = axis_flux(second, second_prim, axis, sign)
        speed = jnp.maximum(
            jnp.abs(first_prim[1][axis]) + sound(first_prim),
            jnp.abs(second_prim[1][axis]) + sound(second_prim),
        )
        hanging = link == base - 1
        for v in range(5):
            star = 0.5 * (first_flux[v] + second_flux[v]) - 0.5 * speed * (second[v] - first[v])
            jump = jnp.where(hanging, 0.0, star) - first_flux[v]
            add_face(sums, v, face, factor * jump)
    from_lanes(sums, out_ref)


def final_kernel(count, back, acc_ref, table_ref, before_ref, after_ref, source_ref, factor_ref, out_ref, pieces, sums):
    elems = acc_ref.shape[2]
    columns = table_ref.shape[1]
    slots = before_ref.shape[1]
    for var in range(5):
        rows = slice(16 * var, 16 * var + 16)
        store_pieces(pieces, 16 * var, slice(0, columns), table_ref[rows, :])
        store_pieces(pieces, 16 * var, slice(columns, columns + slots), before_ref[rows, :])
        store_pieces(
            pieces, 16 * var, slice(columns + slots, columns + 2 * slots), after_ref[rows, :]
        )
    by_lanes(acc_ref, sums)
    factor = -6.0 * factor_ref[...]
    returned = 5 * count + 1
    for face in range(4):
        entry = source_ref[face : face + 1, :]
        beyond = entry - returned
        side = (beyond >= back).astype(jnp.int32)
        spot = jnp.where(
            beyond >= 0, columns + beyond + side * (slots - back), table_column(entry, count)
        )
        star = joined(
            jnp.dot(pieces[...], one_hot(spot, pieces.shape[1]), preferred_element_type=F32)
        )
        for v in range(5):
            add_face(sums, v, face, factor * star[16 * v : 16 * v + 16])
    from_lanes(sums, out_ref)


def body(
    state, step_size, levels, send_faces, partner, mortar_in, mortar_dir, return_faces, flux_source
):
    elems = state.shape[2]
    peers, slots = send_faces.shape
    hop = peers // 2
    count = mortar_dir.shape[0]
    base = 6 * elems + 1
    volume, spread, gather = (jnp.asarray(t) for t in operator_tables())
    factor = (step_size[0] * jnp.exp2(levels.astype(F32) + 1.0)).reshape(1, elems)
    trace = jax.ShapeDtypeStruct((80, slots), F32)
    lanes = pltpu.VMEM((elems // LANES, 320, LANES), F32)

    outgoing = pl.pallas_call(
        send_kernel,
        out_shape=[trace] * peers,
        scratch_shapes=[pltpu.VMEM((240, 6 * elems), BF16), lanes],
    )(state, send_faces)
    arrived = []
    for peer in range(peers):
        distance = peer + 1 if peer < hop else hop - 1 - peer
        arrived.append(passed_along(outgoing[peer], "dev", distance))
    acc, beside, big = pl.pallas_call(
        local_kernel,
        out_shape=[
            jax.ShapeDtypeStruct((5, 64, elems), F32),
            jax.ShapeDtypeStruct((80, 6 * elems), F32),
            jax.ShapeDtypeStruct((80, 5 * LANES), F32),
        ],
        scratch_shapes=[
            pltpu.VMEM((240, 6 * elems), BF16),
            lanes,
            pltpu.VMEM((8, LANES), jnp.int32),
        ],
    )(state, partner, mortar_in, factor, volume)
    table, leave, onward = pl.pallas_call(
        functools.partial(mortar_kernel, base),
        out_shape=[
            jax.ShapeDtypeStruct((80, 5 * LANES), F32),
            jax.ShapeDtypeStruct((80, LANES), F32),
            jax.ShapeDtypeStruct((80, LANES), F32),
        ],
        scratch_shapes=[pltpu.VMEM((240, peers * slots), BF16), pltpu.VMEM((8, LANES), jnp.int32)],
    )(*arrived, big, mortar_in, mortar_dir.reshape(1, count), return_faces, spread, gather)
    before = passed_along(leave, "dev", 1)
    after = passed_along(onward, "dev", -1)
    acc = pl.pallas_call(
        functools.partial(conform_kernel, base),
        out_shape=jax.ShapeDtypeStruct((5, 64, elems), F32),
        scratch_shapes=[pltpu.VMEM((240, peers * slots), BF16), lanes, lanes],
    )(state, partner, factor, acc, beside, *arrived)
    out = pl.pallas_call(
        functools.partial(final_kernel, count, return_faces.shape[1]),
        out_shape=jax.ShapeDtypeStruct((5, 64, elems), F32),
        scratch_shapes=[pltpu.VMEM((240, 7 * LANES), BF16), lanes],
    )(acc, table, before, after, flux_source, factor)
    return out


def solution(mesh):
    placed = (
        P(None, None, "dev"),
        P(),
        P("dev"),
        P("dev", None),
        P(None, "dev"),
        P(None, "dev"),
        P("dev"),
        P("dev", None),
        P(None, "dev"),
    )
    return jax.shard_map(
        body, mesh=mesh, in_specs=placed, out_specs=P(None, None, "dev"), check_vma=False
    )
```

```python
import functools

import jax
import jax.numpy as jnp
import numpy as np
from jax import lax
from jax.experimental import pallas as pl
from jax.experimental.pallas import tpu as pltpu
from jax.sharding import PartitionSpec as P

GAMMA = 1.4
HIGHEST = lax.Precision.HIGHEST
F32 = jnp.float32
BF16 = jnp.bfloat16
LANES = 128


def passed_along(block, axis, distance):
    devices = range(lax.axis_size(axis))
    route = [((i - distance) % len(devices), i) for i in devices]
    return lax.ppermute(block, axis, route)


def lobatto_tables():
    nodes = np.array([-1.0, -1.0 / np.sqrt(5.0), 1.0 / np.sqrt(5.0), 1.0])
    weights = np.array([1.0, 5.0, 5.0, 1.0]) / 6.0

    def basis(points):
        table = np.ones((len(points), 4))
        for column in range(4):
            for other in range(4):
                if other != column:
                    table[:, column] *= (points - nodes[other]) / (nodes[column] - nodes[other])
        return table

    derivative = np.zeros((4, 4))
    for row in range(4):
        for column in range(4):
            total = 0.0
            for other in range(4):
                if other != column:
                    term = 1.0 / (nodes[column] - nodes[other])
                    for third in range(4):
                        if third != column and third != other:
                            term *= (nodes[row] - nodes[third]) / (nodes[column] - nodes[third])
                    total += term
            derivative[row, column] = total
    lower = basis((nodes - 1.0) / 2.0)
    upper = basis((nodes + 1.0) / 2.0)
    back_lower = 0.5 * (lower.T * weights[None, :]) / weights[:, None]
    back_upper = 0.5 * (upper.T * weights[None, :]) / weights[:, None]
    return [
        np.asarray(table, np.float32)
        for table in (derivative, lower, upper, back_lower, back_upper)
    ]


def operator_tables():
    derivative, lower, upper, back_lower, back_upper = lobatto_tables()
    eye = np.eye(4, dtype=np.float32)
    volume = np.concatenate(
        [
            np.kron(derivative, np.kron(eye, eye)),
            np.kron(eye, np.kron(derivative, eye)),
            np.kron(eye, np.kron(eye, derivative)),
        ],
        axis=1,
    )
    five = np.eye(5, dtype=np.float32)
    forward, backward = (lower, upper), (back_lower, back_upper)
    spread = np.concatenate(
        [np.kron(five, np.kron(forward[q % 2], forward[q // 2])) for q in range(4)], axis=0
    )
    gather = np.concatenate(
        [np.kron(five, np.kron(backward[q % 2], backward[q // 2])) for q in range(4)], axis=1
    )
    return volume, spread, gather


def read_lanes(state_hbm, lanes, sems):
    return [
        pltpu.make_async_copy(
            state_hbm.at[:, :, pl.ds(block * LANES, LANES)], lanes.at[block], sems.at[block]
        )
        for block in range(lanes.shape[0])
    ]


def face_part(lanes, block, var, face):
    if face < 2:
        return lanes[block, var, 48 * face : 48 * face + 16, :]
    if face < 4:
        start = 12 * (face % 2)
        return jnp.concatenate(
            [lanes[block, var, 16 * i + start : 16 * i + start + 4, :] for i in range(4)], axis=0
        )
    return lanes[block, var, pl.ds(3 * (face % 2), 16, stride=4), :]


def add_face(lanes, var, face, value):
    for block in range(lanes.shape[0]):
        part = value[:, block * LANES : (block + 1) * LANES]
        if face < 2:
            lanes[block, var, 48 * face : 48 * face + 16, :] += part
        elif face < 4:
            start = 12 * (face % 2)
            for i in range(4):
                lanes[block, var, start + 16 * i : start + 16 * i + 4, :] += part[
                    4 * i : 4 * i + 4
                ]
        else:
            lanes[block, var, pl.ds(3 * (face % 2), 16, stride=4), :] += part


def three_pieces(value):
    high = value.astype(BF16)
    rest = value - high.astype(F32)
    middle = rest.astype(BF16)
    low = (rest - middle.astype(F32)).astype(BF16)
    return high, middle, low


def store_pieces(pieces, rows, columns, value):
    for which, piece in enumerate(three_pieces(value)):
        pieces[80 * which + rows : 80 * which + rows + value.shape[0], columns] = piece


def one_hot(indices, count):
    spots = lax.broadcasted_iota(jnp.int32, (count, indices.shape[1]), 0)
    return (spots == indices).astype(F32).astype(BF16)


def joined(product):
    return (product[0:80] + product[80:160]) + product[160:240]


def primitives(cons):
    inverse = 1.0 / cons[0]
    motion = [cons[1 + axis] * inverse for axis in range(3)]
    pressure = (GAMMA - 1.0) * (
        cons[4] - 0.5 * (cons[1] * motion[0] + cons[2] * motion[1] + cons[3] * motion[2])
    )
    return inverse, motion, pressure


def axis_flux(cons, prim, axis, sign):
    _, motion, pressure = prim
    along = motion[axis] if sign > 0 else -motion[axis]
    push = pressure if sign > 0 else -pressure
    flux = [cons[v] * along for v in range(4)]
    flux[1 + axis] = flux[1 + axis] + push
    flux.append((cons[4] + pressure) * along)
    return flux


def sound(prim):
    inverse, _, pressure = prim
    return jnp.sqrt(GAMMA * pressure * inverse)


def normal_flux(cons, normal):
    inverse, motion, pressure = primitives(cons)
    along = motion[0] * normal[0] + motion[1] * normal[1] + motion[2] * normal[2]
    flux = [
        cons[0] * along,
        cons[1] * along + pressure * normal[0],
        cons[2] * along + pressure * normal[1],
        cons[3] * along + pressure * normal[2],
        (cons[4] + pressure) * along,
    ]
    return flux, jnp.abs(along) + jnp.sqrt(GAMMA * pressure * inverse)


def lane_gather(source, chunk, spots):
    part = source[:, chunk * LANES : (chunk + 1) * LANES]
    return jnp.take_along_axis(part, spots, axis=1)


def packed_places(count):
    return [0, count, 2 * count, LANES, LANES + count]


def lowest(value):
    return jnp.min(value)


def highest(value):
    return jnp.max(value)


def send_kernel(hop, state_hbm, faces_ref, mortar_ref, way_ref, back_ref, *rest):
    peers, slots = faces_ref.shape
    outs = rest[:peers]
    lanes, traces, pieces, table, spots, sems = rest[peers:]
    elems = state_hbm.shape[2]
    chunks = elems // LANES
    count, backs = mortar_ref.shape[1], back_ref.shape[1]
    copies = read_lanes(state_hbm, lanes, sems)
    for copy in copies:
        copy.start()

    wanted = [faces_ref[p : p + 1, :] for p in range(peers)]
    starts, stops = [], []
    for p in range(peers):
        face = sum((wanted[p] >= (k + 1) * elems).astype(jnp.int32) for k in range(6))
        starts.append(lowest(jnp.where(face < 6, face, 5)))
        stops.append(highest(jnp.where(face < 6, face, 0)))
    longest = stops[0] - starts[0]
    for p in range(1, peers):
        longest = jnp.maximum(longest, stops[p] - starts[p])

    table[...] = jnp.zeros(table.shape, F32)
    table[0:5, :] = mortar_ref[...].astype(F32)
    table[5:6, :] = way_ref[...].astype(F32)
    for side in range(2):
        for group in range(4):
            spots[side : side + 1, group * backs : (group + 1) * backs] = back_ref[
                side : side + 1, :
            ]
    lane = lax.broadcasted_iota(jnp.int32, (1, LANES), 1)
    group_of = sum((lane >= (k + 1) * backs).astype(jnp.int32) for k in range(3))
    empty = 6 * elems
    extra = []
    for side, target in ((0, 0), (1, hop)):
        entry = spots[side : side + 1, :]
        kind = sum((entry >= (k + 1) * count).astype(jnp.int32) for k in range(5))
        which = jnp.where(kind < 5, entry - kind * count, -1)
        rows = lax.broadcasted_iota(jnp.int32, (count, LANES), 0)
        found = jnp.dot(
            table[...],
            (rows == which).astype(F32),
            preferred_element_type=F32,
            precision=HIGHEST,
        )
        small = sum(jnp.where(group_of == k, found[1 + k : 2 + k], 0.0) for k in range(4))
        trace = jnp.where(kind == 0, small, found[0:1])
        unused = (kind == 5) | ((kind > 0) & (group_of > 0))
        trace = jnp.where(unused, float(empty), trace).astype(jnp.int32)
        slot = trace - (empty + 1) - (hop if side == 0 else 0) * slots
        code = jnp.where((trace > empty) & (slot >= 0) & (slot < slots), slot, -1)
        outs[target][80:88, slots:] = jnp.zeros((8, LANES), F32)
        outs[target][80:81, slots:] = code.astype(F32)
        outs[target][81:82, slots:] = kind.astype(F32)
        outs[target][82:83, slots:] = found[5:6]
        outs[target][80:88, 0:slots] = jnp.zeros((8, slots), F32)
        extra.append(trace)

    for copy in copies:
        copy.wait()
    for face in range(6):
        for var in range(5):
            for block in range(chunks):
                part = face_part(lanes, block, var, face)
                rows = slice(16 * var, 16 * var + 16)
                columns = slice(block * LANES, (block + 1) * LANES)
                traces[face, rows, columns] = part
                if face < 4:
                    store_pieces(
                        pieces,
                        16 * var,
                        slice(face * elems + block * LANES, face * elems + (block + 1) * LANES),
                        part,
                    )

    def collect(step, first):
        for p in range(peers):
            face = jnp.minimum(starts[p] + step, stops[p])
            local = wanted[p] - face * elems
            chunk_of = jnp.broadcast_to(lax.shift_right_arithmetic(local, 7), (8, LANES))
            spot = jnp.broadcast_to(jnp.bitwise_and(local, LANES - 1), (8, LANES))
            for r in range(10):
                rows = slice(8 * r, 8 * r + 8)
                value = jnp.zeros((8, LANES), F32) if first else outs[p][rows, 0:slots]
                for chunk in range(chunks):
                    part = traces[face, rows, chunk * LANES : (chunk + 1) * LANES]
                    value = jnp.where(
                        chunk_of == chunk, jnp.take_along_axis(part, spot, axis=1), value
                    )
                outs[p][rows, 0:slots] = value

    collect(0, True)
    product = jnp.dot(
        pieces[...],
        one_hot(jnp.concatenate(extra, axis=1), 4 * elems),
        preferred_element_type=F32,
    )
    whole = joined(product)
    outs[0][0:80, slots:] = whole[:, 0:LANES]
    outs[hop][0:80, slots:] = whole[:, LANES:]

    @pl.loop(1, longest + 1)
    def _(step):
        collect(step, False)


def local_kernel(
    state_hbm,
    partner_ref,
    mortar_ref,
    source_ref,
    level_ref,
    step_ref,
    volume_ref,
    acc_ref,
    traces_ref,
    beside_ref,
    big_ref,
    own_ref,
    lanes,
    pieces,
    spots,
    sems,
):
    elems = state_hbm.shape[2]
    chunks = elems // LANES
    count = mortar_ref.shape[1]
    copies = read_lanes(state_hbm, lanes, sems)
    for copy in copies:
        copy.start()
    returned = own_ref.shape[1] // 2
    first_back = 5 * count + 1
    slot = lax.broadcasted_iota(jnp.int32, (returned, elems), 0) + first_back
    number = lax.broadcasted_iota(jnp.int32, (returned, elems), 1)
    hit = jnp.zeros((returned, elems), jnp.int32)
    for face in range(4):
        hit = jnp.where(source_ref[face : face + 1, :] == slot, number + (face * elems + 1), hit)
    column = jnp.sum(hit.astype(F32), axis=1, keepdims=True)
    corner = lax.broadcasted_iota(jnp.int32, (returned, LANES), 0) == lax.broadcasted_iota(
        jnp.int32, (returned, LANES), 1
    )
    owner = jnp.sum(jnp.where(corner, column, 0.0), axis=0, keepdims=True).astype(jnp.int32) - 1
    spots[...] = jnp.full(spots.shape, -1, jnp.int32)
    for row, place in enumerate(packed_places(count)):
        spots[0:1, place : place + count] = mortar_ref[row : row + 1, :]

    for copy in copies:
        copy.wait()
    for face in range(6):
        for var in range(5):
            rows = slice(16 * var, 16 * var + 16)
            for block in range(chunks):
                part = face_part(lanes, block, var, face)
                columns = slice(
                    face * elems + block * LANES, face * elems + (block + 1) * LANES
                )
                traces_ref[rows, columns] = part
                store_pieces(pieces, 16 * var, columns, part)
    for face in range(6):
        other = (face ^ 1) * elems
        product = jnp.dot(
            pieces[:, other : other + elems],
            one_hot(partner_ref[face : face + 1, :] - other, elems),
            preferred_element_type=F32,
        )
        beside_ref[:, face * elems : (face + 1) * elems] = joined(product)
    wanted = spots[0:1, :]
    big_ref[...] = joined(
        jnp.dot(
            pieces[:, 0 : 4 * elems], one_hot(wanted, 4 * elems), preferred_element_type=F32
        )
    )
    own_ref[...] = joined(
        jnp.dot(pieces[:, 0 : 4 * elems], one_hot(owner, 4 * elems), preferred_element_type=F32)
    )
    factor = step_ref[0] * jnp.left_shift(2, level_ref[...]).astype(F32)
    cons = [
        jnp.concatenate([lanes[block, v] for block in range(chunks)], axis=1) for v in range(5)
    ]
    prim = primitives(cons)
    fluxes = [axis_flux(cons, prim, axis, 1) for axis in range(3)]
    for var in range(5):
        stacked = jnp.concatenate([fluxes[axis][var] for axis in range(3)], axis=0)
        total = -factor * jnp.dot(
            volume_ref[...], stacked, preferred_element_type=F32, precision=HIGHEST
        )
        for block in range(chunks):
            acc_ref[block, var] = total[:, block * LANES : (block + 1) * LANES]


def with_reference(traces, empty):
    return jnp.concatenate(
        [
            jnp.where(empty, 1.0, traces[0:16]),
            jnp.where(empty, 0.0, traces[16:64]),
            jnp.where(empty, 2.5, traces[64:80]),
        ],
        axis=0,
    )


def mortar_stars(traces, way, spread, gather):
    normal = [
        (way == 2 * axis + 1).astype(F32) - (way == 2 * axis).astype(F32) for axis in range(3)
    ]
    near = jnp.dot(spread, traces[0], preferred_element_type=F32, precision=HIGHEST)
    stars = []
    for quarter in range(4):
        first = [near[80 * quarter + 16 * v : 80 * quarter + 16 * v + 16] for v in range(5)]
        second = [traces[1 + quarter][16 * v : 16 * v + 16] for v in range(5)]
        first_flux, first_speed = normal_flux(first, normal)
        second_flux, second_speed = normal_flux(second, normal)
        speed = jnp.maximum(first_speed, second_speed)
        stars.append(
            jnp.concatenate(
                [
                    0.5 * (first_flux[v] + second_flux[v]) - 0.5 * speed * (second[v] - first[v])
                    for v in range(5)
                ],
                axis=0,
            )
        )
    whole = jnp.dot(
        gather, jnp.concatenate(stars, axis=0), preferred_element_type=F32, precision=HIGHEST
    )
    return whole, stars


def finish_kernel(base, hop, peers, *rest):
    arrived = rest[:peers]
    (
        acc_ref,
        traces_ref,
        beside_ref,
        big_ref,
        own_ref,
        partner_ref,
        source_ref,
        faces_ref,
        mortar_ref,
        way_ref,
        level_ref,
        step_ref,
        spread_ref,
        gather_ref,
        out_hbm,
        sums,
        outside,
        pieces,
        fluxes,
        payload,
        spots,
        sems,
    ) = rest[peers:]
    slots = faces_ref.shape[1]
    elems = partner_ref.shape[1]
    chunks = elems // LANES
    count = mortar_ref.shape[1]
    empty = base - 1
    wide = 2 * slots
    backs = LANES // 4
    places = packed_places(count)

    links = [partner_ref[face : face + 1, :] for face in range(6)]
    starts, stops = [], []
    for face in range(6):
        block = lax.shift_right_arithmetic(links[face] - base, wide.bit_length() - 1)
        starts.append(lowest(jnp.where(links[face] >= base, block, peers // 2)))
        stops.append(highest(jnp.where(links[face] >= base, block, -1)))
    sources = [source_ref[face : face + 1, :] for face in range(4)]
    farthest = [highest(sources[face]) for face in range(4)]

    for peer in range(peers):
        for var in range(5):
            columns = slice((peer % 2) * slots, (peer % 2 + 1) * slots)
            for which, piece in enumerate(
                three_pieces(arrived[peer][16 * var : 16 * var + 16, 0:slots])
            ):
                row = 80 * which + 16 * var
                pieces[peer // 2, row : row + 16, columns] = piece
    payload[0] = arrived[0][:, slots:]
    payload[1] = arrived[hop][:, slots:]
    codes = [payload[side, 80:81, :] for side in range(2)]

    @pl.when(highest(jnp.maximum(codes[0], codes[1])) >= 0.0)
    def _():
        for side, row in ((0, hop), (1, 0)):
            code = codes[side].astype(jnp.int32)
            listed = jnp.take_along_axis(
                jnp.broadcast_to(faces_ref[row : row + 1, :], (8, LANES)),
                jnp.broadcast_to(jnp.maximum(code, 0), (8, LANES)),
                axis=1,
            )
            listed = jnp.where(jnp.broadcast_to(code, (8, LANES)) >= 0, listed, -1)
            chunk_of = lax.shift_right_arithmetic(listed, 7)
            spot = jnp.bitwise_and(listed, LANES - 1)
            for r in range(10):
                rows = slice(8 * r, 8 * r + 8)

                def pick(chunk, value):
                    start = pl.multiple_of(chunk * LANES, LANES)
                    part = traces_ref[rows, pl.ds(start, LANES)]
                    return jnp.where(
                        chunk_of == chunk, jnp.take_along_axis(part, spot, axis=1), value
                    )

                payload[side, rows, :] = lax.fori_loop(
                    0, 6 * chunks, pick, payload[side, rows, :]
                )

    spots[...] = jnp.full(spots.shape, empty, jnp.int32)
    for row, place in enumerate(places):
        spots[0:1, place : place + count] = mortar_ref[row : row + 1, :]
    spots[1:2, 0:count] = way_ref[...]
    packed = spots[0:1, :]
    total = jnp.zeros((240, wide), F32)
    for block in range(peers // 2):
        total = total + jnp.dot(
            pieces[block],
            one_hot(packed - (base + block * wide), wide),
            preferred_element_type=F32,
        )
    both = with_reference(joined(total) + big_ref[...], packed == empty)
    local = []
    for row, place in enumerate(places):
        part = both[:, 0:LANES] if place < LANES else both[:, LANES:]
        shift = place % LANES
        local.append(part if shift == 0 else pltpu.roll(part, LANES - shift, 1))
    lane = lax.broadcasted_iota(jnp.int32, (1, LANES), 1)
    used = lane < count
    local = [with_reference(part, jnp.logical_not(used)) for part in local]
    local_way = jnp.where(used, spots[1:2, 0:LANES], 0)

    moved = []
    for group in range(4):
        shift = group * backs
        parts = [
            payload[0] if shift == 0 else pltpu.roll(payload[0], LANES - shift, 1),
            payload[1] if shift == backs else pltpu.roll(payload[1], (backs - shift) % LANES, 1),
        ]
        moved.append(jnp.where(lane < backs, parts[0], parts[1]))
    own = own_ref[...]
    unused = (lane >= 2 * backs) | (own[0:1] == 0.0)
    kind = jnp.where(unused, 0, moved[0][81:82].astype(jnp.int32))
    back_way = jnp.where(unused, 0, moved[0][82:83].astype(jnp.int32))
    large = kind == 0
    back = [jnp.where(large, own, moved[0][0:80])]
    for quarter in range(4):
        back.append(jnp.where(large, moved[quarter][0:80], own))
    back = [with_reference(part, unused) for part in back]

    traces = [jnp.concatenate([local[k], back[k]], axis=1) for k in range(5)]
    way = jnp.concatenate([local_way, back_way], axis=1)
    whole, stars = mortar_stars(traces, way, spread_ref[...], gather_ref[...])
    values = [whole[:, 0:LANES]] + [-star[:, 0:LANES] for star in stars]
    result = whole[:, LANES:]
    for quarter in range(4):
        result = jnp.where(kind == 1 + quarter, -stars[quarter][:, LANES:], result)
    halves = [jnp.zeros((80, LANES), F32), jnp.zeros((80, LANES), F32)]
    for row, place in enumerate(places):
        shift = place % LANES
        part = values[row] if shift == 0 else pltpu.roll(values[row], shift, 1)
        inside = (lane >= shift) & (lane < shift + count)
        halves[place // LANES] = jnp.where(inside, part, halves[place // LANES])
    for which, value in enumerate(halves + [result]):
        store_pieces(fluxes, 0, slice(which * LANES, (which + 1) * LANES), value[0:16])
        for var in range(1, 5):
            store_pieces(
                fluxes,
                16 * var,
                slice(which * LANES, (which + 1) * LANES),
                value[16 * var : 16 * var + 16],
            )

    sums[...] = acc_ref[...]
    factor = (-6.0 * step_ref[0]) * jnp.left_shift(2, level_ref[...]).astype(F32)
    for face in range(6):
        axis, sign = face // 2, 2 * (face % 2) - 1
        columns = slice(face * elems, (face + 1) * elems)
        outside[...] = beside_ref[:, columns]

        @pl.loop(starts[face], stops[face] + 1)
        def _(block, face=face):
            outside[...] += joined(
                jnp.dot(
                    pieces[block],
                    one_hot(links[face] - base - block * wide, wide),
                    preferred_element_type=F32,
                )
            )

        first = [traces_ref[16 * v : 16 * v + 16, columns] for v in range(5)]
        second = [outside[16 * v : 16 * v + 16, :] for v in range(5)]
        first_prim, second_prim = primitives(first), primitives(second)
        first_flux = axis_flux(first, first_prim, axis, sign)
        second_flux = axis_flux(second, second_prim, axis, sign)
        speed = jnp.maximum(
            jnp.abs(first_prim[1][axis]) + sound(first_prim),
            jnp.abs(second_prim[1][axis]) + sound(second_prim),
        )
        hanging = links[face] == empty
        for v in range(5):
            star = 0.5 * (first_flux[v] + second_flux[v]) - 0.5 * speed * (second[v] - first[v])
            jump = jnp.where(hanging, 0.0, star) - first_flux[v]
            add_face(sums, v, face, factor * jump)
        if face < 4:
            entry = sources[face]
            row = sum((entry >= (k + 1) * count).astype(jnp.int32) for k in range(4))
            spot = entry - row * count
            column = jnp.where(row >= 3, LANES + (row - 3) * count, row * count) + spot
            column = jnp.where(entry < 5 * count, column, -1)

            @pl.when(highest(jnp.where(entry == 5 * count, -1, entry)) >= 0)
            def _(face=face, column=column):
                star = joined(
                    jnp.dot(
                        fluxes[:, 0 : 2 * LANES],
                        one_hot(column, 2 * LANES),
                        preferred_element_type=F32,
                    )
                )
                for v in range(5):
                    add_face(sums, v, face, factor * star[16 * v : 16 * v + 16])

            @pl.when(farthest[face] > 5 * count)
            def _(face=face, entry=entry):
                star = joined(
                    jnp.dot(
                        fluxes[:, 2 * LANES :],
                        one_hot(entry - (5 * count + 1), LANES),
                        preferred_element_type=F32,
                    )
                )
                for v in range(5):
                    add_face(sums, v, face, factor * star[16 * v : 16 * v + 16])

    copies = [
        pltpu.make_async_copy(
            sums.at[block], out_hbm.at[:, :, pl.ds(block * LANES, LANES)], sems.at[block]
        )
        for block in range(chunks)
    ]
    for copy in copies:
        copy.start()
    for copy in copies:
        copy.wait()


def body(
    state, step_size, levels, send_faces, partner, mortar_in, mortar_dir, return_faces, flux_source
):
    elems = state.shape[2]
    peers, slots = send_faces.shape
    hop = peers // 2
    count = mortar_dir.shape[0]
    base = 6 * elems + 1
    chunks = elems // LANES
    if slots != LANES or 4 * return_faces.shape[1] != LANES or 3 * count > LANES:
        raise ValueError("sizes")
    volume, spread, gather = (jnp.asarray(t) for t in operator_tables())
    way = mortar_dir.reshape(1, count)
    level = levels.reshape(1, elems)
    vmem = pl.BlockSpec(memory_space=pltpu.VMEM)
    smem = pl.BlockSpec(memory_space=pltpu.SMEM)
    hbm = pl.BlockSpec(memory_space=pl.ANY)
    lanes = pltpu.VMEM((chunks, 5, 64, LANES), F32)
    sems = pltpu.SemaphoreType.DMA((chunks,))

    shapes = [
        jax.ShapeDtypeStruct((88, 2 * slots) if p in (0, hop) else (80, slots), F32)
        for p in range(peers)
    ]
    outgoing = pl.pallas_call(
        functools.partial(send_kernel, hop),
        out_shape=shapes,
        in_specs=[hbm] + [vmem] * 4,
        out_specs=[vmem] * peers,
        scratch_shapes=[
            lanes,
            pltpu.VMEM((6, 80, elems), F32),
            pltpu.VMEM((240, 4 * elems), BF16),
            pltpu.VMEM((8, count), F32),
            pltpu.VMEM((8, LANES), jnp.int32),
            sems,
        ],
        name="send",
    )(state, send_faces, mortar_in, way, return_faces)
    arrived = []
    for peer in range(peers):
        distance = peer + 1 if peer < hop else hop - 1 - peer
        arrived.append(passed_along(outgoing[peer], "dev", distance))
    acc, traces, beside, big, own = pl.pallas_call(
        local_kernel,
        out_shape=[
            jax.ShapeDtypeStruct((chunks, 5, 64, LANES), F32),
            jax.ShapeDtypeStruct((80, 6 * elems), F32),
            jax.ShapeDtypeStruct((80, 6 * elems), F32),
            jax.ShapeDtypeStruct((80, 2 * LANES), F32),
            jax.ShapeDtypeStruct((80, LANES), F32),
        ],
        in_specs=[hbm] + [vmem] * 4 + [smem, vmem],
        out_specs=[vmem] * 5,
        scratch_shapes=[
            lanes,
            pltpu.VMEM((240, 6 * elems), BF16),
            pltpu.VMEM((8, 2 * LANES), jnp.int32),
            sems,
        ],
        name="local",
    )(state, partner, mortar_in, flux_source, level, step_size, volume)
    return pl.pallas_call(
        functools.partial(finish_kernel, base, hop, peers),
        out_shape=jax.ShapeDtypeStruct((5, 64, elems), F32),
        in_specs=[vmem] * (peers + 11) + [smem, vmem, vmem],
        out_specs=hbm,
        scratch_shapes=[
            lanes,
            pltpu.VMEM((80, elems), F32),
            pltpu.VMEM((peers // 2, 240, 2 * slots), BF16),
            pltpu.VMEM((240, 3 * LANES), BF16),
            pltpu.VMEM((2, 88, LANES), F32),
            pltpu.VMEM((8, 2 * LANES), jnp.int32),
            sems,
        ],
        name="finish",
    )(
        *arrived,
        acc,
        traces,
        beside,
        big,
        own,
        partner,
        flux_source,
        send_faces,
        mortar_in,
        way,
        level,
        step_size,
        spread,
        gather,
    )


def solution(mesh):
    placed = (
        P(None, None, "dev"),
        P(),
        P("dev"),
        P("dev", None),
        P(None, "dev"),
        P(None, "dev"),
        P("dev"),
        P("dev", None),
        P(None, "dev"),
    )
    return jax.shard_map(
        body, mesh=mesh, in_specs=placed, out_specs=P(None, None, "dev"), check_vma=False
    )
```

```python
import functools

import jax
import jax.numpy as jnp
import numpy as np
from jax import lax
from jax.experimental import pallas as pl
from jax.experimental.pallas import tpu as pltpu
from jax.sharding import PartitionSpec as P


GAMMA = 1.4
HIGHEST = lax.Precision.HIGHEST
F32 = jnp.float32
BF16 = jnp.bfloat16
LANES = 128


def passed_along(block, axis, distance):
    devices = range(lax.axis_size(axis))
    route = [((i - distance) % len(devices), i) for i in devices]
    return lax.ppermute(block, axis, route)


def lobatto_tables():
    nodes = np.array([-1.0, -1.0 / np.sqrt(5.0), 1.0 / np.sqrt(5.0), 1.0])
    weights = np.array([1.0, 5.0, 5.0, 1.0]) / 6.0

    def basis(points):
        table = np.ones((len(points), 4))
        for column in range(4):
            for other in range(4):
                if other != column:
                    table[:, column] *= (points - nodes[other]) / (nodes[column] - nodes[other])
        return table

    derivative = np.zeros((4, 4))
    for row in range(4):
        for column in range(4):
            total = 0.0
            for other in range(4):
                if other != column:
                    term = 1.0 / (nodes[column] - nodes[other])
                    for third in range(4):
                        if third != column and third != other:
                            term *= (nodes[row] - nodes[third]) / (nodes[column] - nodes[third])
                    total += term
            derivative[row, column] = total
    lower = basis((nodes - 1.0) / 2.0)
    upper = basis((nodes + 1.0) / 2.0)
    back_lower = 0.5 * (lower.T * weights[None, :]) / weights[:, None]
    back_upper = 0.5 * (upper.T * weights[None, :]) / weights[:, None]
    return [
        np.asarray(table, np.float32)
        for table in (derivative, lower, upper, back_lower, back_upper)
    ]


def operator_tables():
    derivative, lower, upper, back_lower, back_upper = lobatto_tables()
    eye = np.eye(4, dtype=np.float32)
    volume = np.concatenate(
        [
            np.kron(derivative, np.kron(eye, eye)),
            np.kron(eye, np.kron(derivative, eye)),
            np.kron(eye, np.kron(eye, derivative)),
        ],
        axis=1,
    )
    five = np.eye(5, dtype=np.float32)
    forward, backward = (lower, upper), (back_lower, back_upper)
    spread = np.concatenate(
        [np.kron(five, np.kron(forward[q % 2], forward[q // 2])) for q in range(4)], axis=0
    )
    gather = np.concatenate(
        [np.kron(five, np.kron(backward[q % 2], backward[q // 2])) for q in range(4)], axis=1
    )
    return volume, spread, gather


def split_table(table):
    kind = jnp.dtype(BF16)
    high = table.astype(kind)
    rest = table - high.astype(np.float32)
    middle = rest.astype(kind)
    return high, middle, (rest - middle.astype(np.float32)).astype(kind)


def read_lanes(state_hbm, lanes, sems):
    return [
        pltpu.make_async_copy(
            state_hbm.at[:, :, pl.ds(block * LANES, LANES)], lanes.at[block], sems.at[block]
        )
        for block in range(lanes.shape[0])
    ]


def face_part(lanes, block, var, face):
    if face < 2:
        return lanes[block, var, 48 * face : 48 * face + 16, :]
    if face < 4:
        start = 12 * (face % 2)
        return jnp.concatenate(
            [lanes[block, var, 16 * i + start : 16 * i + start + 4, :] for i in range(4)], axis=0
        )
    return lanes[block, var, pl.ds(3 * (face % 2), 16, stride=4), :]


def add_face(lanes, var, face, value):
    for block in range(lanes.shape[0]):
        part = value[:, block * LANES : (block + 1) * LANES]
        if face < 2:
            lanes[block, var, 48 * face : 48 * face + 16, :] += part
        elif face < 4:
            start = 12 * (face % 2)
            for i in range(4):
                lanes[block, var, start + 16 * i : start + 16 * i + 4, :] += part[
                    4 * i : 4 * i + 4
                ]
        else:
            lanes[block, var, pl.ds(3 * (face % 2), 16, stride=4), :] += part


def three_pieces(value):
    high = value.astype(BF16)
    rest = value - high.astype(F32)
    middle = rest.astype(BF16)
    low = (rest - middle.astype(F32)).astype(BF16)
    return high, middle, low


def store_pieces(pieces, rows, columns, value):
    for which, piece in enumerate(three_pieces(value)):
        pieces[80 * which + rows : 80 * which + rows + value.shape[0], columns] = piece


ROWS = 512


def number_rows(grid):
    grid[...] = lax.broadcasted_iota(jnp.int32, grid.shape, 0).astype(jnp.int16)


def one_hot(grid, indices, count):
    width = indices.shape[1]
    rows = min(count, ROWS)
    row = jnp.broadcast_to(indices, (16, width)).astype(jnp.int16)
    spots = jnp.concatenate([grid[0:rows, :]] * (width // LANES), axis=1)
    parts = []
    for start in range(0, count, rows):
        want = jnp.concatenate([row - jnp.int16(start)] * (rows // 16), axis=0)
        parts.append(jnp.where(spots == want, jnp.ones((), BF16), jnp.zeros((), BF16)))
    return parts[0] if len(parts) == 1 else jnp.concatenate(parts, axis=0)


def joined(product):
    return (product[0:80] + product[80:160]) + product[160:240]


def primitives(cons):
    inverse = 1.0 / cons[0]
    motion = [cons[1 + axis] * inverse for axis in range(3)]
    pressure = (GAMMA - 1.0) * (
        cons[4] - 0.5 * (cons[1] * motion[0] + cons[2] * motion[1] + cons[3] * motion[2])
    )
    return inverse, motion, pressure


def axis_flux(cons, prim, axis, sign):
    _, motion, pressure = prim
    along = motion[axis] if sign > 0 else -motion[axis]
    push = pressure if sign > 0 else -pressure
    flux = [cons[v] * along for v in range(4)]
    flux[1 + axis] = flux[1 + axis] + push
    flux.append((cons[4] + pressure) * along)
    return flux


def sound(prim):
    inverse, _, pressure = prim
    return jnp.sqrt(GAMMA * pressure * inverse)


def normal_flux(cons, normal):
    inverse, motion, pressure = primitives(cons)
    along = motion[0] * normal[0] + motion[1] * normal[1] + motion[2] * normal[2]
    flux = [
        cons[0] * along,
        cons[1] * along + pressure * normal[0],
        cons[2] * along + pressure * normal[1],
        cons[3] * along + pressure * normal[2],
        (cons[4] + pressure) * along,
    ]
    return flux, jnp.abs(along) + jnp.sqrt(GAMMA * pressure * inverse)


def packed_places(count):
    return [0, count, 2 * count, LANES, LANES + count]


def highest(value):
    return jnp.max(value)


def send_kernel(hop, state_hbm, faces_ref, mortar_ref, way_ref, back_ref, *rest):
    peers, slots = faces_ref.shape
    outs = rest[:peers]
    lanes, traces, pieces, table, spots, grid, sems = rest[peers:]
    elems = state_hbm.shape[2]
    chunks = elems // LANES
    count, backs = mortar_ref.shape[1], back_ref.shape[1]
    copies = read_lanes(state_hbm, lanes, sems)
    for copy in copies:
        copy.start()

    wanted = [faces_ref[p : p + 1, :] for p in range(peers)]
    faces = faces_ref[...]
    face = sum((faces >= (k + 1) * elems).astype(jnp.int32) for k in range(6))
    least = jnp.min(jnp.where(face < 6, face, 5), axis=1, keepdims=True)
    most = jnp.max(jnp.where(face < 6, face, 0), axis=1, keepdims=True)
    longest = highest(most - least)
    starts = [least[p, 0] for p in range(peers)]
    stops = [most[p, 0] for p in range(peers)]

    number_rows(grid)
    table[...] = jnp.zeros(table.shape, F32)
    table[0:5, :] = mortar_ref[...].astype(F32)
    table[5:6, :] = way_ref[...].astype(F32)
    for side in range(2):
        for group in range(4):
            spots[side : side + 1, group * backs : (group + 1) * backs] = back_ref[
                side : side + 1, :
            ]
    lane = lax.broadcasted_iota(jnp.int32, (1, LANES), 1)
    group_of = sum((lane >= (k + 1) * backs).astype(jnp.int32) for k in range(3))
    empty = 6 * elems
    extra = []
    for side, target in ((0, 0), (1, hop)):
        entry = spots[side : side + 1, :]
        kind = sum((entry >= (k + 1) * count).astype(jnp.int32) for k in range(5))
        which = jnp.where(kind < 5, entry - kind * count, -1)
        rows = lax.broadcasted_iota(jnp.int32, (count, LANES), 0)
        found = jnp.dot(
            table[...],
            (rows == which).astype(F32),
            preferred_element_type=F32,
            precision=HIGHEST,
        )
        small = sum(jnp.where(group_of == k, found[1 + k : 2 + k], 0.0) for k in range(4))
        trace = jnp.where(kind == 0, small, found[0:1])
        unused = (kind == 5) | ((kind > 0) & (group_of > 0))
        trace = jnp.where(unused, float(empty), trace).astype(jnp.int32)
        slot = trace - (empty + 1) - (hop if side == 0 else 0) * slots
        code = jnp.where((trace > empty) & (slot >= 0) & (slot < slots), slot, -1)
        outs[target][80:88, slots:] = jnp.zeros((8, LANES), F32)
        outs[target][80:81, slots:] = code.astype(F32)
        outs[target][81:82, slots:] = kind.astype(F32)
        outs[target][82:83, slots:] = found[5:6]
        outs[target][80:88, 0:slots] = jnp.zeros((8, slots), F32)
        extra.append(trace)

    for copy in copies:
        copy.wait()
    for face in range(6):
        for var in range(5):
            for block in range(chunks):
                part = face_part(lanes, block, var, face)
                rows = slice(16 * var, 16 * var + 16)
                columns = slice(block * LANES, (block + 1) * LANES)
                traces[face, rows, columns] = part
                if face < 4:
                    store_pieces(
                        pieces,
                        16 * var,
                        slice(face * elems + block * LANES, face * elems + (block + 1) * LANES),
                        part,
                    )

    def collect(step, first):
        for p in range(peers):
            face = jnp.minimum(starts[p] + step, stops[p])
            local = wanted[p] - face * elems
            chunk_of = jnp.broadcast_to(lax.shift_right_arithmetic(local, 7), (8, LANES))
            spot = jnp.broadcast_to(jnp.bitwise_and(local, LANES - 1), (8, LANES))
            for r in range(10):
                rows = slice(8 * r, 8 * r + 8)
                value = jnp.zeros((8, LANES), F32) if first else outs[p][rows, 0:slots]
                for chunk in range(chunks):
                    part = traces[face, rows, chunk * LANES : (chunk + 1) * LANES]
                    value = jnp.where(
                        chunk_of == chunk, jnp.take_along_axis(part, spot, axis=1), value
                    )
                outs[p][rows, 0:slots] = value

    collect(0, True)
    product = jnp.dot(
        pieces[...],
        one_hot(grid, jnp.concatenate(extra, axis=1), 4 * elems),
        preferred_element_type=F32,
    )
    whole = joined(product)
    outs[0][0:80, slots:] = whole[:, 0:LANES]
    outs[hop][0:80, slots:] = whole[:, LANES:]

    @pl.loop(1, longest + 1)
    def _(step):
        collect(step, False)


def local_kernel(
    block_count,
    state_hbm,
    partner_ref,
    mortar_ref,
    source_ref,
    level_ref,
    step_ref,
    volume_ref,
    acc_ref,
    traces_ref,
    beside_ref,
    big_ref,
    own_ref,
    range_ref,
    lanes,
    pieces,
    spots,
    grid,
    sems,
):
    elems = state_hbm.shape[2]
    chunks = elems // LANES
    count = mortar_ref.shape[1]
    wide = 2 * LANES
    number_rows(grid)
    links = partner_ref[...]
    block = lax.shift_right_arithmetic(links - (6 * elems + 1), wide.bit_length() - 1)
    least = jnp.min(jnp.where(block >= 0, block, block_count), axis=1, keepdims=True)
    most = jnp.max(block, axis=1, keepdims=True)
    for face in range(6):
        range_ref[face] = jnp.minimum(least[face, 0], block_count - 1)
        range_ref[8 + face] = most[face, 0]
    range_ref[6] = highest(jnp.where(most > least, 1, 0))
    copies = read_lanes(state_hbm, lanes, sems)
    for copy in copies:
        copy.start()
    returned = own_ref.shape[1] // 2
    first_back = 5 * count + 1
    slot = lax.broadcasted_iota(jnp.int32, (returned, elems), 0) + first_back
    number = lax.broadcasted_iota(jnp.int32, (returned, elems), 1)
    hit = jnp.zeros((returned, elems), jnp.int32)
    for face in range(4):
        hit = jnp.where(source_ref[face : face + 1, :] == slot, number + (face * elems + 1), hit)
    column = jnp.sum(hit.astype(F32), axis=1, keepdims=True)
    corner = lax.broadcasted_iota(jnp.int32, (returned, LANES), 0) == lax.broadcasted_iota(
        jnp.int32, (returned, LANES), 1
    )
    owner = jnp.sum(jnp.where(corner, column, 0.0), axis=0, keepdims=True).astype(jnp.int32) - 1
    spots[...] = jnp.full(spots.shape, -1, jnp.int32)
    for row, place in enumerate(packed_places(count)):
        spots[0:1, place : place + count] = mortar_ref[row : row + 1, :]

    for copy in copies:
        copy.wait()
    for face in range(6):
        for var in range(5):
            rows = slice(16 * var, 16 * var + 16)
            for block in range(chunks):
                part = face_part(lanes, block, var, face)
                columns = slice(
                    face * elems + block * LANES, face * elems + (block + 1) * LANES
                )
                traces_ref[rows, columns] = part
                store_pieces(pieces, 16 * var, columns, part)
    for face in range(6):
        other = (face ^ 1) * elems
        product = jnp.dot(
            pieces[:, other : other + elems],
            one_hot(grid, partner_ref[face : face + 1, :] - other, elems),
            preferred_element_type=F32,
        )
        beside_ref[:, face * elems : (face + 1) * elems] = joined(product)
    wanted = spots[0:1, :]
    big_ref[...] = joined(
        jnp.dot(
            pieces[:, 0 : 4 * elems], one_hot(grid, wanted, 4 * elems), preferred_element_type=F32
        )
    )
    own_ref[...] = joined(
        jnp.dot(pieces[:, 0 : 4 * elems], one_hot(grid, owner, 4 * elems), preferred_element_type=F32)
    )
    factor = -step_ref[0] * jnp.left_shift(2, level_ref[...]).astype(F32)
    cons = [
        jnp.concatenate([lanes[block, v] for block in range(chunks)], axis=1) for v in range(5)
    ]
    prim = primitives(cons)
    fluxes = [axis_flux(cons, prim, axis, 1) for axis in range(3)]
    for var in range(5):
        stacked = jnp.concatenate([fluxes[axis][var] for axis in range(3)], axis=0)
        high, middle, low = three_pieces(stacked)
        first = jnp.dot(volume_ref[...], high, preferred_element_type=F32)
        second = jnp.dot(volume_ref[0:128, :], middle, preferred_element_type=F32)
        third = jnp.dot(volume_ref[0:64, :], low, preferred_element_type=F32)
        total = factor * (
            first[0:64]
            + ((first[64:128] + second[0:64]) + ((first[128:192] + second[64:128]) + third))
        )
        for block in range(chunks):
            acc_ref[block, var] = total[:, block * LANES : (block + 1) * LANES]


def with_reference(traces, empty):
    return jnp.concatenate(
        [
            jnp.where(empty, 1.0, traces[0:16]),
            jnp.where(empty, 0.0, traces[16:64]),
            jnp.where(empty, 2.5, traces[64:80]),
        ],
        axis=0,
    )


def mortar_stars(traces, way, spread, gather):
    normal = [
        (way == 2 * axis + 1).astype(F32) - (way == 2 * axis).astype(F32) for axis in range(3)
    ]
    near = jnp.dot(spread, traces[0], preferred_element_type=F32, precision=HIGHEST)
    stars = []
    for quarter in range(4):
        first = [near[80 * quarter + 16 * v : 80 * quarter + 16 * v + 16] for v in range(5)]
        second = [traces[1 + quarter][16 * v : 16 * v + 16] for v in range(5)]
        first_flux, first_speed = normal_flux(first, normal)
        second_flux, second_speed = normal_flux(second, normal)
        speed = jnp.maximum(first_speed, second_speed)
        stars.append(
            jnp.concatenate(
                [
                    0.5 * (first_flux[v] + second_flux[v]) - 0.5 * speed * (second[v] - first[v])
                    for v in range(5)
                ],
                axis=0,
            )
        )
    whole = jnp.dot(
        gather, jnp.concatenate(stars, axis=0), preferred_element_type=F32, precision=HIGHEST
    )
    return whole, stars


def finish_kernel(base, hop, peers, *rest):
    arrived = rest[:peers]
    (
        acc_ref,
        traces_ref,
        beside_ref,
        big_ref,
        own_ref,
        partner_ref,
        source_ref,
        faces_ref,
        mortar_ref,
        way_ref,
        level_ref,
        step_ref,
        spread_ref,
        gather_ref,
        range_ref,
        out_hbm,
        sums,
        outside,
        pieces,
        fluxes,
        stars_of,
        payload,
        spots,
        grid,
        sems,
    ) = rest[peers:]
    slots = faces_ref.shape[1]
    elems = partner_ref.shape[1]
    chunks = elems // LANES
    count = mortar_ref.shape[1]
    empty = base - 1
    wide = 2 * slots
    backs = LANES // 4
    places = packed_places(count)

    number_rows(grid)
    links = [partner_ref[face : face + 1, :] for face in range(6)]
    sources = [source_ref[face : face + 1, :] for face in range(4)]

    for peer in range(peers):
        for var in range(5):
            columns = slice((peer % 2) * slots, (peer % 2 + 1) * slots)
            for which, piece in enumerate(
                three_pieces(arrived[peer][16 * var : 16 * var + 16, 0:slots])
            ):
                row = 80 * which + 16 * var
                pieces[peer // 2, row : row + 16, columns] = piece
    payload[0] = arrived[0][:, slots:]
    payload[1] = arrived[hop][:, slots:]
    codes = [payload[side, 80:81, :] for side in range(2)]

    @pl.when(highest(jnp.maximum(codes[0], codes[1])) >= 0.0)
    def _():
        for side, row in ((0, hop), (1, 0)):
            code = codes[side].astype(jnp.int32)
            listed = jnp.take_along_axis(
                jnp.broadcast_to(faces_ref[row : row + 1, :], (8, LANES)),
                jnp.broadcast_to(jnp.maximum(code, 0), (8, LANES)),
                axis=1,
            )
            listed = jnp.where(jnp.broadcast_to(code, (8, LANES)) >= 0, listed, -1)
            chunk_of = lax.shift_right_arithmetic(listed, 7)
            spot = jnp.bitwise_and(listed, LANES - 1)
            for r in range(10):
                rows = slice(8 * r, 8 * r + 8)

                def pick(chunk, value):
                    start = pl.multiple_of(chunk * LANES, LANES)
                    part = traces_ref[rows, pl.ds(start, LANES)]
                    return jnp.where(
                        chunk_of == chunk, jnp.take_along_axis(part, spot, axis=1), value
                    )

                payload[side, rows, :] = lax.fori_loop(
                    0, 6 * chunks, pick, payload[side, rows, :]
                )

    @pl.when(range_ref[6] == 0)
    def _():
        outside[...] = jnp.zeros(outside.shape, F32)

    @pl.when(range_ref[6] != 0)
    def _():
        for face in range(6):
            outside[face] = jnp.zeros(outside.shape[1:], F32)

            @pl.loop(range_ref[face] + 1, range_ref[8 + face] + 1)
            def _(block, face=face):
                outside[face] += joined(
                    jnp.dot(
                        pieces[block],
                        one_hot(grid, links[face] - base - block * wide, wide),
                        preferred_element_type=F32,
                    )
                )

    factor = (-6.0 * step_ref[0]) * jnp.left_shift(2, level_ref[...]).astype(F32)
    sums[...] = acc_ref[...]
    for face in range(6):
        axis, sign = face // 2, 2 * (face % 2) - 1
        columns = slice(face * elems, (face + 1) * elems)
        block = range_ref[face]
        near = joined(
            jnp.dot(
                pieces[block],
                one_hot(grid, links[face] - base - block * wide, wide),
                preferred_element_type=F32,
            )
        )
        near = near + (beside_ref[:, columns] + outside[face])
        first = [traces_ref[16 * v : 16 * v + 16, columns] for v in range(5)]
        second = [near[16 * v : 16 * v + 16, :] for v in range(5)]
        first_prim, second_prim = primitives(first), primitives(second)
        first_flux = axis_flux(first, first_prim, axis, sign)
        second_flux = axis_flux(second, second_prim, axis, sign)
        speed = jnp.maximum(
            jnp.abs(first_prim[1][axis]) + sound(first_prim),
            jnp.abs(second_prim[1][axis]) + sound(second_prim),
        )
        hanging = links[face] == empty
        for v in range(5):
            star = 0.5 * (second_flux[v] - first_flux[v]) - 0.5 * speed * (second[v] - first[v])
            jump = jnp.where(hanging, -first_flux[v], star)
            if face < 4:
                stars_of[face, 16 * v : 16 * v + 16, :] = jump
            else:
                add_face(sums, v, face, factor * jump)

    spots[...] = jnp.full(spots.shape, empty, jnp.int32)
    for row, place in enumerate(places):
        spots[0:1, place : place + count] = mortar_ref[row : row + 1, :]
    spots[1:2, 0:count] = way_ref[...]
    packed = spots[0:1, :]
    total = jnp.zeros((240, wide), F32)
    for block in range(peers // 2):
        total = total + jnp.dot(
            pieces[block],
            one_hot(grid, packed - (base + block * wide), wide),
            preferred_element_type=F32,
        )
    both = with_reference(joined(total) + big_ref[...], packed == empty)
    local = []
    for row, place in enumerate(places):
        part = both[:, 0:LANES] if place < LANES else both[:, LANES:]
        shift = place % LANES
        local.append(part if shift == 0 else pltpu.roll(part, LANES - shift, 1))
    lane = lax.broadcasted_iota(jnp.int32, (1, LANES), 1)
    used = lane < count
    local = [with_reference(part, jnp.logical_not(used)) for part in local]
    local_way = jnp.where(used, spots[1:2, 0:LANES], 0)

    moved = []
    for group in range(4):
        shift = group * backs
        parts = [
            payload[0] if shift == 0 else pltpu.roll(payload[0], LANES - shift, 1),
            payload[1] if shift == backs else pltpu.roll(payload[1], (backs - shift) % LANES, 1),
        ]
        moved.append(jnp.where(lane < backs, parts[0], parts[1]))
    own = own_ref[...]
    unused = (lane >= 2 * backs) | (own[0:1] == 0.0)
    kind = jnp.where(unused, 0, moved[0][81:82].astype(jnp.int32))
    back_way = jnp.where(unused, 0, moved[0][82:83].astype(jnp.int32))
    large = kind == 0
    back = [jnp.where(large, own, moved[0][0:80])]
    for quarter in range(4):
        back.append(jnp.where(large, moved[quarter][0:80], own))
    back = [with_reference(part, unused) for part in back]

    traces = [jnp.concatenate([local[k], back[k]], axis=1) for k in range(5)]
    way = jnp.concatenate([local_way, back_way], axis=1)
    whole, stars = mortar_stars(traces, way, spread_ref[...], gather_ref[...])
    values = [whole[:, 0:LANES]] + [-star[:, 0:LANES] for star in stars]
    result = whole[:, LANES:]
    for quarter in range(4):
        result = jnp.where(kind == 1 + quarter, -stars[quarter][:, LANES:], result)
    halves = [jnp.zeros((80, LANES), F32), jnp.zeros((80, LANES), F32)]
    for row, place in enumerate(places):
        shift = place % LANES
        part = values[row] if shift == 0 else pltpu.roll(values[row], shift, 1)
        inside = (lane >= shift) & (lane < shift + count)
        halves[place // LANES] = jnp.where(inside, part, halves[place // LANES])
    for which, value in enumerate(halves + [result]):
        store_pieces(fluxes, 0, slice(which * LANES, (which + 1) * LANES), value[0:16])
        for var in range(1, 5):
            store_pieces(
                fluxes,
                16 * var,
                slice(which * LANES, (which + 1) * LANES),
                value[16 * var : 16 * var + 16],
            )

    for face in range(4):
        entry = sources[face]
        row = sum((entry >= (k + 1) * count).astype(jnp.int32) for k in range(4))
        spot = entry - row * count
        column = jnp.where(row >= 3, LANES + (row - 3) * count, row * count) + spot
        beyond = 2 * LANES + entry - (5 * count + 1)
        column = jnp.where(entry < 5 * count, column, jnp.where(entry > 5 * count, beyond, -1))
        star = joined(
            jnp.dot(
                fluxes[...], one_hot(grid, column, 3 * LANES), preferred_element_type=F32
            )
        )
        for v in range(5):
            rows = slice(16 * v, 16 * v + 16)
            add_face(sums, v, face, factor * (stars_of[face, rows, :] + star[rows, :]))

    copies = [
        pltpu.make_async_copy(
            sums.at[block], out_hbm.at[:, :, pl.ds(block * LANES, LANES)], sems.at[block]
        )
        for block in range(chunks)
    ]
    for copy in copies:
        copy.start()
    for copy in copies:
        copy.wait()


def body(
    state, step_size, levels, send_faces, partner, mortar_in, mortar_dir, return_faces, flux_source
):
    elems = state.shape[2]
    peers, slots = send_faces.shape
    hop = peers // 2
    count = mortar_dir.shape[0]
    base = 6 * elems + 1
    chunks = elems // LANES
    if slots != LANES or 4 * return_faces.shape[1] != LANES or 3 * count > LANES:
        raise ValueError("sizes")
    volume, spread, gather = operator_tables()
    volume = jnp.asarray(np.concatenate(split_table(volume), axis=0))
    spread, gather = jnp.asarray(spread), jnp.asarray(gather)
    way = mortar_dir.reshape(1, count)
    level = levels.reshape(1, elems)
    vmem = pl.BlockSpec(memory_space=pltpu.VMEM)
    smem = pl.BlockSpec(memory_space=pltpu.SMEM)
    hbm = pl.BlockSpec(memory_space=pl.ANY)
    lanes = pltpu.VMEM((chunks, 5, 64, LANES), F32)
    sems = pltpu.SemaphoreType.DMA((chunks,))
    grid = pltpu.VMEM((ROWS, LANES), jnp.int16)

    shapes = [
        jax.ShapeDtypeStruct((88, 2 * slots) if p in (0, hop) else (80, slots), F32)
        for p in range(peers)
    ]
    outgoing = pl.pallas_call(
        functools.partial(send_kernel, hop),
        out_shape=shapes,
        in_specs=[hbm] + [vmem] * 4,
        out_specs=[vmem] * peers,
        scratch_shapes=[
            lanes,
            pltpu.VMEM((6, 80, elems), F32),
            pltpu.VMEM((240, 4 * elems), BF16),
            pltpu.VMEM((8, count), F32),
            pltpu.VMEM((8, LANES), jnp.int32),
            grid,
            sems,
        ],
        name="send",
    )(state, send_faces, mortar_in, way, return_faces)
    arrived = []
    for peer in range(peers):
        distance = peer + 1 if peer < hop else hop - 1 - peer
        arrived.append(passed_along(outgoing[peer], "dev", distance))
    acc, traces, beside, big, own, ranges = pl.pallas_call(
        functools.partial(local_kernel, peers // 2),
        out_shape=[
            jax.ShapeDtypeStruct((chunks, 5, 64, LANES), F32),
            jax.ShapeDtypeStruct((80, 6 * elems), F32),
            jax.ShapeDtypeStruct((80, 6 * elems), F32),
            jax.ShapeDtypeStruct((80, 2 * LANES), F32),
            jax.ShapeDtypeStruct((80, LANES), F32),
            jax.ShapeDtypeStruct((16,), jnp.int32),
        ],
        in_specs=[hbm] + [vmem] * 4 + [smem, vmem],
        out_specs=[vmem] * 5 + [smem],
        scratch_shapes=[
            lanes,
            pltpu.VMEM((240, 6 * elems), BF16),
            pltpu.VMEM((8, 2 * LANES), jnp.int32),
            grid,
            sems,
        ],
        name="local",
    )(state, partner, mortar_in, flux_source, level, step_size, volume)
    return pl.pallas_call(
        functools.partial(finish_kernel, base, hop, peers),
        out_shape=jax.ShapeDtypeStruct((5, 64, elems), F32),
        in_specs=[vmem] * (peers + 11) + [smem, vmem, vmem, smem],
        out_specs=hbm,
        scratch_shapes=[
            lanes,
            pltpu.VMEM((6, 80, elems), F32),
            pltpu.VMEM((peers // 2, 240, 2 * slots), BF16),
            pltpu.VMEM((240, 3 * LANES), BF16),
            pltpu.VMEM((4, 80, elems), F32),
            pltpu.VMEM((2, 88, LANES), F32),
            pltpu.VMEM((8, 2 * LANES), jnp.int32),
            grid,
            sems,
        ],
        name="finish",
    )(
        *arrived,
        acc,
        traces,
        beside,
        big,
        own,
        partner,
        flux_source,
        send_faces,
        mortar_in,
        way,
        level,
        step_size,
        spread,
        gather,
        ranges,
    )


def solution(mesh):
    placed = (
        P(None, None, "dev"),
        P(),
        P("dev"),
        P("dev", None),
        P(None, "dev"),
        P(None, "dev"),
        P("dev"),
        P("dev", None),
        P(None, "dev"),
    )

    return jax.shard_map(
        body, mesh=mesh, in_specs=placed, out_specs=P(None, None, "dev"), check_vma=False
    )
```

```python
import functools

import jax
import jax.numpy as jnp
import numpy as np
from jax import lax
from jax.experimental import pallas as pl
from jax.experimental.pallas import tpu as pltpu
from jax.sharding import PartitionSpec as P


GAMMA = 1.4
HIGHEST = lax.Precision.HIGHEST
F32 = jnp.float32
BF16 = jnp.bfloat16
LANES = 128


def passed_along(block, axis, distance):
    devices = range(lax.axis_size(axis))
    route = [((i - distance) % len(devices), i) for i in devices]
    return lax.ppermute(block, axis, route)


def lobatto_tables():
    nodes = np.array([-1.0, -1.0 / np.sqrt(5.0), 1.0 / np.sqrt(5.0), 1.0])
    weights = np.array([1.0, 5.0, 5.0, 1.0]) / 6.0

    def basis(points):
        table = np.ones((len(points), 4))
        for column in range(4):
            for other in range(4):
                if other != column:
                    table[:, column] *= (points - nodes[other]) / (nodes[column] - nodes[other])
        return table

    derivative = np.zeros((4, 4))
    for row in range(4):
        for column in range(4):
            total = 0.0
            for other in range(4):
                if other != column:
                    term = 1.0 / (nodes[column] - nodes[other])
                    for third in range(4):
                        if third != column and third != other:
                            term *= (nodes[row] - nodes[third]) / (nodes[column] - nodes[third])
                    total += term
            derivative[row, column] = total
    lower = basis((nodes - 1.0) / 2.0)
    upper = basis((nodes + 1.0) / 2.0)
    back_lower = 0.5 * (lower.T * weights[None, :]) / weights[:, None]
    back_upper = 0.5 * (upper.T * weights[None, :]) / weights[:, None]
    return [
        np.asarray(table, np.float32)
        for table in (derivative, lower, upper, back_lower, back_upper)
    ]


def operator_tables():
    derivative, lower, upper, back_lower, back_upper = lobatto_tables()
    eye = np.eye(4, dtype=np.float32)
    volume = np.concatenate(
        [
            np.kron(derivative, np.kron(eye, eye)),
            np.kron(eye, np.kron(derivative, eye)),
            np.kron(eye, np.kron(eye, derivative)),
        ],
        axis=1,
    )
    five = np.eye(5, dtype=np.float32)
    forward, backward = (lower, upper), (back_lower, back_upper)
    spread = np.concatenate(
        [np.kron(five, np.kron(forward[q % 2], forward[q // 2])) for q in range(4)], axis=0
    )
    gather = np.concatenate(
        [np.kron(five, np.kron(backward[q % 2], backward[q // 2])) for q in range(4)], axis=1
    )
    return volume, spread, gather


def split_table(table):
    kind = jnp.dtype(BF16)
    high = table.astype(kind)
    rest = table - high.astype(np.float32)
    middle = rest.astype(kind)
    return high, middle, (rest - middle.astype(np.float32)).astype(kind)


def read_lanes(state_hbm, lanes, sems):
    return [
        pltpu.make_async_copy(
            state_hbm.at[:, :, pl.ds(block * LANES, LANES)], lanes.at[block], sems.at[block]
        )
        for block in range(lanes.shape[0])
    ]


def face_part(lanes, block, var, face):
    if face < 2:
        return lanes[block, var, 48 * face : 48 * face + 16, :]
    if face < 4:
        start = 12 * (face % 2)
        return jnp.concatenate(
            [lanes[block, var, 16 * i + start : 16 * i + start + 4, :] for i in range(4)], axis=0
        )
    return lanes[block, var, pl.ds(3 * (face % 2), 16, stride=4), :]


def add_face(lanes, var, face, value):
    for block in range(lanes.shape[0]):
        part = value[:, block * LANES : (block + 1) * LANES]
        if face < 2:
            lanes[block, var, 48 * face : 48 * face + 16, :] += part
        elif face < 4:
            start = 12 * (face % 2)
            for i in range(4):
                lanes[block, var, start + 16 * i : start + 16 * i + 4, :] += part[
                    4 * i : 4 * i + 4
                ]
        else:
            lanes[block, var, pl.ds(3 * (face % 2), 16, stride=4), :] += part


def three_pieces(value):
    high = value.astype(BF16)
    rest = value - high.astype(F32)
    middle = rest.astype(BF16)
    low = (rest - middle.astype(F32)).astype(BF16)
    return high, middle, low


def store_pieces(pieces, rows, columns, value):
    for which, piece in enumerate(three_pieces(value)):
        pieces[80 * which + rows : 80 * which + rows + value.shape[0], columns] = piece


ROWS = 512


def number_rows(grid):
    grid[...] = lax.broadcasted_iota(jnp.int32, grid.shape, 0).astype(jnp.int16)


def one_hot(grid, indices, count):
    width = indices.shape[1]
    rows = min(count, ROWS)
    row = jnp.broadcast_to(indices, (16, width)).astype(jnp.int16)
    spots = jnp.concatenate([grid[0:rows, :]] * (width // LANES), axis=1)
    parts = []
    for start in range(0, count, rows):
        want = jnp.concatenate([row - jnp.int16(start)] * (rows // 16), axis=0)
        parts.append(jnp.where(spots == want, jnp.ones((), BF16), jnp.zeros((), BF16)))
    return parts[0] if len(parts) == 1 else jnp.concatenate(parts, axis=0)


def split_product(table_ref, value):
    rows = table_ref.shape[0] // 3
    high, middle, low = three_pieces(value)
    first = jnp.dot(table_ref[...], high, preferred_element_type=F32)
    second = jnp.dot(table_ref[0 : 2 * rows, :], middle, preferred_element_type=F32)
    third = jnp.dot(table_ref[0:rows, :], low, preferred_element_type=F32)
    small = (first[2 * rows :] + second[rows:]) + third
    return first[0:rows] + ((first[rows : 2 * rows] + second[0:rows]) + small)


def joined(product):
    return (product[0:80] + product[80:160]) + product[160:240]


def primitives(cons):
    inverse = 1.0 / cons[0]
    motion = [cons[1 + axis] * inverse for axis in range(3)]
    pressure = (GAMMA - 1.0) * (
        cons[4] - 0.5 * (cons[1] * motion[0] + cons[2] * motion[1] + cons[3] * motion[2])
    )
    return inverse, motion, pressure


def axis_flux(cons, prim, axis, sign):
    _, motion, pressure = prim
    along = motion[axis] if sign > 0 else -motion[axis]
    push = pressure if sign > 0 else -pressure
    flux = [cons[v] * along for v in range(4)]
    flux[1 + axis] = flux[1 + axis] + push
    flux.append((cons[4] + pressure) * along)
    return flux


def sound(prim):
    inverse, _, pressure = prim
    return jnp.sqrt(GAMMA * pressure * inverse)


def normal_flux(cons, normal):
    inverse, motion, pressure = primitives(cons)
    along = motion[0] * normal[0] + motion[1] * normal[1] + motion[2] * normal[2]
    flux = [
        cons[0] * along,
        cons[1] * along + pressure * normal[0],
        cons[2] * along + pressure * normal[1],
        cons[3] * along + pressure * normal[2],
        (cons[4] + pressure) * along,
    ]
    return flux, jnp.abs(along) + jnp.sqrt(GAMMA * pressure * inverse)


def packed_places(count):
    return [0, count, 2 * count, LANES, LANES + count]


def highest(value):
    return jnp.max(value)


def send_kernel(hop, peers, *rest):
    inputs, outs, held = rest[:11], rest[11 : 11 + peers], rest[11 + peers : 21 + peers]
    traces, pieces, table, spots, grid, back_ref, sems, state_sems = rest[21 + peers :]
    lanes, faces_ref, mortar_ref, way_ref = held[:4]
    elems = inputs[0].shape[2]
    chunks = elems // LANES
    targets = [faces_ref, mortar_ref, way_ref, back_ref] + list(held[4:])
    loads = [
        pltpu.make_async_copy(source, target, sems.at[k])
        for k, (source, target) in enumerate(zip(inputs[1:], targets))
    ]
    copies = read_lanes(inputs[0], lanes, state_sems)
    for copy in loads[:4] + copies + loads[4:]:
        copy.start()
    slots = faces_ref.shape[1]
    count, backs = mortar_ref.shape[1], back_ref.shape[1]
    number_rows(grid)
    for copy in loads[:4]:
        copy.wait()

    wanted = [faces_ref[p : p + 1, :] for p in range(peers)]
    faces = faces_ref[...]
    face = sum((faces >= (k + 1) * elems).astype(jnp.int32) for k in range(6))
    least = jnp.min(jnp.where(face < 6, face, 5), axis=1, keepdims=True)
    most = jnp.max(jnp.where(face < 6, face, 0), axis=1, keepdims=True)
    longest = highest(most - least)
    starts = [least[p, 0] for p in range(peers)]
    stops = [most[p, 0] for p in range(peers)]

    table[...] = jnp.zeros(table.shape, F32)
    table[0:5, :] = mortar_ref[...].astype(F32)
    table[5:6, :] = way_ref[...].astype(F32)
    for side in range(2):
        for group in range(4):
            spots[side : side + 1, group * backs : (group + 1) * backs] = back_ref[
                side : side + 1, :
            ]
    lane = lax.broadcasted_iota(jnp.int32, (1, LANES), 1)
    group_of = sum((lane >= (k + 1) * backs).astype(jnp.int32) for k in range(3))
    empty = 6 * elems
    extra = []
    for side, target in ((0, 0), (1, hop)):
        entry = spots[side : side + 1, :]
        kind = sum((entry >= (k + 1) * count).astype(jnp.int32) for k in range(5))
        which = jnp.where(kind < 5, entry - kind * count, -1)
        rows = lax.broadcasted_iota(jnp.int32, (count, LANES), 0)
        found = jnp.dot(
            table[...],
            (rows == which).astype(F32),
            preferred_element_type=F32,
            precision=HIGHEST,
        )
        small = sum(jnp.where(group_of == k, found[1 + k : 2 + k], 0.0) for k in range(4))
        trace = jnp.where(kind == 0, small, found[0:1])
        unused = (kind == 5) | ((kind > 0) & (group_of > 0))
        trace = jnp.where(unused, float(empty), trace).astype(jnp.int32)
        slot = trace - (empty + 1) - (hop if side == 0 else 0) * slots
        code = jnp.where((trace > empty) & (slot >= 0) & (slot < slots), slot, -1)
        outs[target][80:88, slots:] = jnp.zeros((8, LANES), F32)
        outs[target][80:81, slots:] = code.astype(F32)
        outs[target][81:82, slots:] = kind.astype(F32)
        outs[target][82:83, slots:] = found[5:6]
        outs[target][80:88, 0:slots] = jnp.zeros((8, slots), F32)
        extra.append(trace)

    for copy in copies:
        copy.wait()
    for face in range(6):
        for var in range(5):
            for block in range(chunks):
                part = face_part(lanes, block, var, face)
                rows = slice(16 * var, 16 * var + 16)
                columns = slice(block * LANES, (block + 1) * LANES)
                traces[face, rows, columns] = part
                if face < 4:
                    store_pieces(
                        pieces,
                        16 * var,
                        slice(face * elems + block * LANES, face * elems + (block + 1) * LANES),
                        part,
                    )

    def collect(step, first):
        for p in range(peers):
            face = jnp.minimum(starts[p] + step, stops[p])
            local = wanted[p] - face * elems
            chunk_of = jnp.broadcast_to(lax.shift_right_arithmetic(local, 7), (8, LANES))
            spot = jnp.broadcast_to(jnp.bitwise_and(local, LANES - 1), (8, LANES))
            for r in range(10):
                rows = slice(8 * r, 8 * r + 8)
                value = jnp.zeros((8, LANES), F32) if first else outs[p][rows, 0:slots]
                for chunk in range(chunks):
                    part = traces[face, rows, chunk * LANES : (chunk + 1) * LANES]
                    value = jnp.where(
                        chunk_of == chunk, jnp.take_along_axis(part, spot, axis=1), value
                    )
                outs[p][rows, 0:slots] = value

    collect(0, True)
    product = jnp.dot(
        pieces[...],
        one_hot(grid, jnp.concatenate(extra, axis=1), 4 * elems),
        preferred_element_type=F32,
    )
    whole = joined(product)
    outs[0][0:80, slots:] = whole[:, 0:LANES]
    outs[hop][0:80, slots:] = whole[:, LANES:]

    @pl.loop(1, longest + 1)
    def _(step):
        collect(step, False)

    for copy in loads[4:]:
        copy.wait()


def local_kernel(
    block_count,
    lanes,
    partner_ref,
    mortar_ref,
    source_ref,
    level_ref,
    volume_ref,
    acc_ref,
    traces_ref,
    beside_ref,
    big_ref,
    own_ref,
    range_ref,
    pieces,
    spots,
    grid,
):
    elems = partner_ref.shape[1]
    chunks = elems // LANES
    count = mortar_ref.shape[1]
    wide = 2 * LANES
    number_rows(grid)
    links = partner_ref[...]
    block = lax.shift_right_arithmetic(links - (6 * elems + 1), wide.bit_length() - 1)
    least = jnp.min(jnp.where(block >= 0, block, block_count), axis=1, keepdims=True)
    most = jnp.max(block, axis=1, keepdims=True)
    for face in range(6):
        range_ref[face] = jnp.minimum(least[face, 0], block_count - 1)
        range_ref[8 + face] = most[face, 0]
    range_ref[6] = highest(jnp.where(most > least, 1, 0))
    returned = own_ref.shape[1] // 2
    first_back = 5 * count + 1
    slot = lax.broadcasted_iota(jnp.int32, (returned, elems), 0) + first_back
    number = lax.broadcasted_iota(jnp.int32, (returned, elems), 1)
    hit = jnp.zeros((returned, elems), jnp.int32)
    for face in range(4):
        hit = jnp.where(source_ref[face : face + 1, :] == slot, number + (face * elems + 1), hit)
    column = jnp.sum(hit.astype(F32), axis=1, keepdims=True)
    corner = lax.broadcasted_iota(jnp.int32, (returned, LANES), 0) + count == (
        lax.broadcasted_iota(jnp.int32, (returned, LANES), 1)
    )
    owner = jnp.sum(jnp.where(corner, column, 0.0), axis=0, keepdims=True).astype(jnp.int32) - 1
    spots[...] = jnp.full(spots.shape, -1, jnp.int32)
    for row, place in enumerate(packed_places(count)):
        spots[0:1, place : place + count] = mortar_ref[row : row + 1, :]

    for face in range(6):
        for var in range(5):
            rows = slice(16 * var, 16 * var + 16)
            for block in range(chunks):
                part = face_part(lanes, block, var, face)
                columns = slice(
                    face * elems + block * LANES, face * elems + (block + 1) * LANES
                )
                traces_ref[rows, columns] = part
                if face < 4:
                    store_pieces(pieces, 16 * var, columns, part)

    def lane_gathered(wanted, first, last, out, column):
        spot = jnp.broadcast_to(jnp.bitwise_and(wanted, LANES - 1), (8, LANES))
        chunk_of = jnp.broadcast_to(lax.shift_right_arithmetic(wanted, 7), (8, LANES))
        for r in range(10):
            rows = slice(8 * r, 8 * r + 8)
            value = jnp.zeros((8, LANES), F32)
            for chunk in range(first, last):
                part = traces_ref[rows, chunk * LANES : (chunk + 1) * LANES]
                value = jnp.where(
                    chunk_of == chunk, jnp.take_along_axis(part, spot, axis=1), value
                )
            out[rows, column : column + LANES] = value

    def matrix_gathered(face):
        other = (face ^ 1) * elems
        product = jnp.dot(
            pieces[:, other : other + elems],
            one_hot(grid, partner_ref[face : face + 1, :] - other, elems),
            preferred_element_type=F32,
        )
        beside_ref[:, face * elems : (face + 1) * elems] = joined(product)

    wanted = spots[0:1, :]
    for face in range(4):
        matrix_gathered(face)
        if face < 2:
            for block in range(chunks):
                columns = slice(block * LANES, (block + 1) * LANES)
                first = ((4 + face) ^ 1) * chunks
                lane_gathered(
                    partner_ref[4 + face : 5 + face, columns],
                    first,
                    first + chunks,
                    beside_ref,
                    (4 + face) * elems + block * LANES,
                )
        if face == 2:
            lane_gathered(owner, 0, 4 * chunks, own_ref, 0)
    big_ref[...] = joined(
        jnp.dot(pieces[...], one_hot(grid, wanted, 4 * elems), preferred_element_type=F32)
    )
    factor = -(jnp.left_shift(2, level_ref[...]).astype(F32))
    cons = [
        jnp.concatenate([lanes[block, v] for block in range(chunks)], axis=1) for v in range(5)
    ]
    prim = primitives(cons)
    fluxes = [axis_flux(cons, prim, axis, 1) for axis in range(3)]
    for var in range(5):
        stacked = jnp.concatenate([fluxes[axis][var] for axis in range(3)], axis=0)
        total = factor * split_product(volume_ref, stacked)
        for block in range(chunks):
            acc_ref[block, var] = total[:, block * LANES : (block + 1) * LANES]


def with_reference(traces, empty):
    return jnp.concatenate(
        [
            jnp.where(empty, 1.0, traces[0:16]),
            jnp.where(empty, 0.0, traces[16:64]),
            jnp.where(empty, 2.5, traces[64:80]),
        ],
        axis=0,
    )


def finish_kernel(base, hop, peers, *rest):
    arrived = rest[:peers]
    (
        acc_ref,
        traces_ref,
        beside_ref,
        big_ref,
        own_ref,
        partner_ref,
        source_ref,
        faces_ref,
        mortar_ref,
        way_ref,
        level_ref,
        step_ref,
        spread_ref,
        gather_ref,
        range_ref,
        out_hbm,
        sums,
        outside,
        pieces,
        fluxes,
        stars_of,
        payload,
        spots,
        grid,
        sems,
    ) = rest[peers:]
    slots = faces_ref.shape[1]
    elems = partner_ref.shape[1]
    chunks = elems // LANES
    count = mortar_ref.shape[1]
    empty = base - 1
    wide = 2 * slots
    backs = LANES // 4
    places = packed_places(count)

    number_rows(grid)
    links = [partner_ref[face : face + 1, :] for face in range(6)]
    sources = [source_ref[face : face + 1, :] for face in range(4)]

    for peer in range(peers):
        for var in range(5):
            columns = slice((peer % 2) * slots, (peer % 2 + 1) * slots)
            for which, piece in enumerate(
                three_pieces(arrived[peer][16 * var : 16 * var + 16, 0:slots])
            ):
                row = 80 * which + 16 * var
                pieces[peer // 2, row : row + 16, columns] = piece
    payload[0] = arrived[0][:, slots:]
    payload[1] = arrived[hop][:, slots:]
    codes = [payload[side, 80:81, :] for side in range(2)]

    @pl.when(highest(jnp.maximum(codes[0], codes[1])) >= 0.0)
    def _():
        for side, row in ((0, hop), (1, 0)):
            code = codes[side].astype(jnp.int32)
            listed = jnp.take_along_axis(
                jnp.broadcast_to(faces_ref[row : row + 1, :], (8, LANES)),
                jnp.broadcast_to(jnp.maximum(code, 0), (8, LANES)),
                axis=1,
            )
            listed = jnp.where(jnp.broadcast_to(code, (8, LANES)) >= 0, listed, -1)
            chunk_of = lax.shift_right_arithmetic(listed, 7)
            spot = jnp.bitwise_and(listed, LANES - 1)
            for r in range(10):
                rows = slice(8 * r, 8 * r + 8)

                def pick(chunk, value):
                    start = pl.multiple_of(chunk * LANES, LANES)
                    part = traces_ref[rows, pl.ds(start, LANES)]
                    return jnp.where(
                        chunk_of == chunk, jnp.take_along_axis(part, spot, axis=1), value
                    )

                payload[side, rows, :] = lax.fori_loop(
                    0, 6 * chunks, pick, payload[side, rows, :]
                )

    @pl.when(range_ref[6] == 0)
    def _():
        outside[...] = jnp.zeros(outside.shape, F32)

    @pl.when(range_ref[6] != 0)
    def _():
        for face in range(6):
            outside[face] = jnp.zeros(outside.shape[1:], F32)

            @pl.loop(range_ref[face] + 1, range_ref[8 + face] + 1)
            def _(block, face=face):
                outside[face] += joined(
                    jnp.dot(
                        pieces[block],
                        one_hot(grid, links[face] - base - block * wide, wide),
                        preferred_element_type=F32,
                    )
                )

    factor = (-6.0 * step_ref[0]) * jnp.left_shift(2, level_ref[...]).astype(F32)
    sums[...] = step_ref[0] * acc_ref[...]

    def conform(face):
        axis, sign = face // 2, 2 * (face % 2) - 1
        columns = slice(face * elems, (face + 1) * elems)
        block = range_ref[face]
        near = joined(
            jnp.dot(
                pieces[block],
                one_hot(grid, links[face] - base - block * wide, wide),
                preferred_element_type=F32,
            )
        )
        near = near + (beside_ref[:, columns] + outside[face])
        first = [traces_ref[16 * v : 16 * v + 16, columns] for v in range(5)]
        second = [near[16 * v : 16 * v + 16, :] for v in range(5)]
        first_prim, second_prim = primitives(first), primitives(second)
        first_flux = axis_flux(first, first_prim, axis, sign)
        second_flux = axis_flux(second, second_prim, axis, sign)
        speed = jnp.maximum(
            jnp.abs(first_prim[1][axis]) + sound(first_prim),
            jnp.abs(second_prim[1][axis]) + sound(second_prim),
        )
        hanging = links[face] == empty
        for v in range(5):
            star = 0.5 * (second_flux[v] - first_flux[v]) - 0.5 * speed * (second[v] - first[v])
            jump = jnp.where(hanging, -first_flux[v], star)
            if face < 4:
                stars_of[face, 16 * v : 16 * v + 16, :] = jump
            else:
                add_face(sums, v, face, factor * jump)

    def mortar():
        spots[...] = jnp.full(spots.shape, empty, jnp.int32)
        for row, place in enumerate(places):
            spots[0:1, place : place + count] = mortar_ref[row : row + 1, :]
        spots[1:2, 0:count] = way_ref[...]
        packed = spots[0:1, :]
        total = jnp.zeros((240, wide), F32)
        for block in range(peers // 2):
            total = total + jnp.dot(
                pieces[block],
                one_hot(grid, packed - (base + block * wide), wide),
                preferred_element_type=F32,
            )
        both = joined(total) + big_ref[...]
        yield
        lane = lax.broadcasted_iota(jnp.int32, (1, LANES), 1)
        mine = lane < count
        backs_end = count + 2 * backs
        own = own_ref[...]
        moved = []
        for group in range(4):
            shift = group * backs
            parts = [
                pltpu.roll(payload[side], (count + side * backs - shift) % LANES, 1)
                for side in range(2)
            ]
            moved.append(jnp.where(lane < count + backs, parts[0], parts[1]))
        unused = (lane >= backs_end) | ((lane >= count) & (own[0:1] == 0.0))
        unused = unused | (mine & (packed[:, 0:LANES] == empty))
        kind = jnp.where(mine, 0, moved[0][81:82].astype(jnp.int32))
        way = jnp.where(mine, spots[1:2, 0:LANES], moved[0][82:83].astype(jnp.int32))
        large = kind == 0
        traces = []
        for row, place in enumerate(places):
            part = both[:, 0:LANES] if place < LANES else both[:, LANES:]
            shift = place % LANES
            part = part if shift == 0 else pltpu.roll(part, LANES - shift, 1)
            if row == 0:
                back = jnp.where(large, own, moved[0][0:80])
            else:
                back = jnp.where(large, moved[row - 1][0:80], own)
            traces.append(with_reference(jnp.where(mine, part, back), unused))
        normal = [
            (way == 2 * axis + 1).astype(F32) - (way == 2 * axis).astype(F32) for axis in range(3)
        ]
        near = split_product(spread_ref, traces[0])
        yield
        stars = []
        for quarter in range(4):
            first = [near[80 * quarter + 16 * v : 80 * quarter + 16 * v + 16] for v in range(5)]
            second = [traces[1 + quarter][16 * v : 16 * v + 16] for v in range(5)]
            first_flux, first_speed = normal_flux(first, normal)
            second_flux, second_speed = normal_flux(second, normal)
            speed = jnp.maximum(first_speed, second_speed)
            stars.append(
                jnp.concatenate(
                    [
                        0.5 * (first_flux[v] + second_flux[v])
                        - 0.5 * speed * (second[v] - first[v])
                        for v in range(5)
                    ],
                    axis=0,
                )
            )
            if quarter == 1:
                yield
        whole = split_product(gather_ref, jnp.concatenate(stars, axis=0))
        yield
        values = [whole] + [-star for star in stars]
        result = whole
        for quarter in range(4):
            result = jnp.where(kind == 1 + quarter, values[1 + quarter], result)
        halves = [jnp.zeros((80, LANES), F32), jnp.zeros((80, LANES), F32)]
        for row, place in enumerate(places):
            shift = place % LANES
            part = values[row] if shift == 0 else pltpu.roll(values[row], shift, 1)
            inside = (lane >= shift) & (lane < shift + count)
            halves[place // LANES] = jnp.where(inside, part, halves[place // LANES])
        for which, value in enumerate(halves + [result]):
            columns = slice(which * LANES, (which + 1) * LANES)
            for var in range(5):
                store_pieces(fluxes, 16 * var, columns, value[16 * var : 16 * var + 16])

    chain = mortar()
    for face in (4, 5, 0, 1, 2, 3):
        next(chain, None)
        conform(face)
    for _ in chain:
        pass

    for face in range(4):
        entry = sources[face]
        row = sum((entry >= (k + 1) * count).astype(jnp.int32) for k in range(4))
        spot = entry - row * count
        column = jnp.where(row >= 3, LANES + (row - 3) * count, row * count) + spot
        beyond = 2 * LANES + count + entry - (5 * count + 1)
        column = jnp.where(entry < 5 * count, column, jnp.where(entry > 5 * count, beyond, -1))
        star = joined(
            jnp.dot(
                fluxes[...], one_hot(grid, column, 3 * LANES), preferred_element_type=F32
            )
        )
        for v in range(5):
            rows = slice(16 * v, 16 * v + 16)
            add_face(sums, v, face, factor * (stars_of[face, rows, :] + star[rows, :]))

    copies = [
        pltpu.make_async_copy(
            sums.at[block], out_hbm.at[:, :, pl.ds(block * LANES, LANES)], sems.at[block]
        )
        for block in range(chunks)
    ]
    for copy in copies:
        copy.start()
    for copy in copies:
        copy.wait()


def body(
    state, step_size, levels, send_faces, partner, mortar_in, mortar_dir, return_faces, flux_source
):
    elems = state.shape[2]
    peers, slots = send_faces.shape
    hop = peers // 2
    count = mortar_dir.shape[0]
    base = 6 * elems + 1
    chunks = elems // LANES
    backs = return_faces.shape[1]
    if slots != LANES or 4 * backs != LANES or max(3 * count, count + 2 * backs) > LANES:
        raise ValueError("sizes")
    volume, spread, gather = (
        jnp.asarray(np.concatenate(split_table(t), axis=0)) for t in operator_tables()
    )
    way = mortar_dir.reshape(1, count)
    level = levels.reshape(1, elems)
    vmem = pl.BlockSpec(memory_space=pltpu.VMEM)
    smem = pl.BlockSpec(memory_space=pltpu.SMEM)
    hbm = pl.BlockSpec(memory_space=pltpu.HBM)
    lanes = jax.ShapeDtypeStruct((chunks, 5, 64, LANES), F32)
    sems = pltpu.SemaphoreType.DMA((chunks,))
    grid = pltpu.VMEM((ROWS, LANES), jnp.int16)

    shapes = [
        jax.ShapeDtypeStruct((88, 2 * slots) if p in (0, hop) else (80, slots), F32)
        for p in range(peers)
    ]
    inputs = [state, send_faces, mortar_in, way, return_faces, partner, flux_source, level]
    inputs += [volume, spread, gather]
    held = [lanes] + [
        jax.ShapeDtypeStruct(x.shape, x.dtype) for x in inputs[1:4] + inputs[5:]
    ]
    results = pl.pallas_call(
        functools.partial(send_kernel, hop, peers),
        out_shape=shapes + held,
        in_specs=[hbm] * len(inputs),
        out_specs=[vmem] * (peers + len(held)),
        scratch_shapes=[
            pltpu.VMEM((6, 80, elems), F32),
            pltpu.VMEM((240, 4 * elems), BF16),
            pltpu.VMEM((8, count), F32),
            pltpu.VMEM((8, LANES), jnp.int32),
            grid,
            pltpu.VMEM(return_faces.shape, jnp.int32),
            pltpu.SemaphoreType.DMA((len(inputs) - 1,)),
            sems,
        ],
        name="send",
        compiler_params=pltpu.CompilerParams(vmem_limit_bytes=14 << 20),
    )(*[pltpu.with_memory_space_constraint(x, pltpu.HBM) for x in inputs])
    outgoing = results[:peers]
    state, send_faces, mortar_in, way, partner, flux_source, level = results[peers : peers + 7]
    volume, spread, gather = results[peers + 7 :]
    arrived = []
    for peer in range(peers):
        distance = peer + 1 if peer < hop else hop - 1 - peer
        arrived.append(passed_along(outgoing[peer], "dev", distance))
    acc, traces, beside, big, own, ranges = pl.pallas_call(
        functools.partial(local_kernel, peers // 2),
        out_shape=[
            lanes,
            jax.ShapeDtypeStruct((80, 6 * elems), F32),
            jax.ShapeDtypeStruct((80, 6 * elems), F32),
            jax.ShapeDtypeStruct((80, 2 * LANES), F32),
            jax.ShapeDtypeStruct((80, LANES), F32),
            jax.ShapeDtypeStruct((16,), jnp.int32),
        ],
        in_specs=[vmem] * 6,
        out_specs=[vmem] * 5 + [smem],
        scratch_shapes=[
            pltpu.VMEM((240, 4 * elems), BF16),
            pltpu.VMEM((8, 2 * LANES), jnp.int32),
            grid,
        ],
        name="local",
        compiler_params=pltpu.CompilerParams(vmem_limit_bytes=14 << 20),
    )(state, partner, mortar_in, flux_source, level, volume)
    return pl.pallas_call(
        functools.partial(finish_kernel, base, hop, peers),
        out_shape=jax.ShapeDtypeStruct((5, 64, elems), F32),
        in_specs=[vmem] * (peers + 11) + [smem, vmem, vmem, smem],
        out_specs=hbm,
        scratch_shapes=[
            pltpu.VMEM(lanes.shape, F32),
            pltpu.VMEM((6, 80, elems), F32),
            pltpu.VMEM((peers // 2, 240, 2 * slots), BF16),
            pltpu.VMEM((240, 3 * LANES), BF16),
            pltpu.VMEM((4, 80, elems), F32),
            pltpu.VMEM((2, 88, LANES), F32),
            pltpu.VMEM((8, 2 * LANES), jnp.int32),
            grid,
            sems,
        ],
        name="finish",
        compiler_params=pltpu.CompilerParams(vmem_limit_bytes=14 << 20),
    )(
        *arrived,
        acc,
        traces,
        beside,
        big,
        own,
        partner,
        flux_source,
        send_faces,
        mortar_in,
        way,
        level,
        step_size,
        spread,
        gather,
        ranges,
    )


def solution(mesh):
    placed = (
        P(None, None, "dev"),
        P(),
        P("dev"),
        P("dev", None),
        P(None, "dev"),
        P(None, "dev"),
        P("dev"),
        P("dev", None),
        P(None, "dev"),
    )

    return jax.shard_map(
        body, mesh=mesh, in_specs=placed, out_specs=P(None, None, "dev"), check_vma=False
    )
```

```python
import functools

import jax
import jax.numpy as jnp
import numpy as np
from jax import lax
from jax.experimental import pallas as pl
from jax.experimental.pallas import tpu as pltpu
from jax.sharding import PartitionSpec as P


GAMMA = 1.4
HIGHEST = lax.Precision.HIGHEST
F32 = jnp.float32
BF16 = jnp.bfloat16
LANES = 128


def passed_along(block, axis, distance):
    devices = range(lax.axis_size(axis))
    route = [((i - distance) % len(devices), i) for i in devices]
    return lax.ppermute(block, axis, route)


def lobatto_tables():
    nodes = np.array([-1.0, -1.0 / np.sqrt(5.0), 1.0 / np.sqrt(5.0), 1.0])
    weights = np.array([1.0, 5.0, 5.0, 1.0]) / 6.0

    def basis(points):
        table = np.ones((len(points), 4))
        for column in range(4):
            for other in range(4):
                if other != column:
                    table[:, column] *= (points - nodes[other]) / (nodes[column] - nodes[other])
        return table

    derivative = np.zeros((4, 4))
    for row in range(4):
        for column in range(4):
            total = 0.0
            for other in range(4):
                if other != column:
                    term = 1.0 / (nodes[column] - nodes[other])
                    for third in range(4):
                        if third != column and third != other:
                            term *= (nodes[row] - nodes[third]) / (nodes[column] - nodes[third])
                    total += term
            derivative[row, column] = total
    lower = basis((nodes - 1.0) / 2.0)
    upper = basis((nodes + 1.0) / 2.0)
    back_lower = 0.5 * (lower.T * weights[None, :]) / weights[:, None]
    back_upper = 0.5 * (upper.T * weights[None, :]) / weights[:, None]
    return [
        np.asarray(table, np.float32)
        for table in (derivative, lower, upper, back_lower, back_upper)
    ]


def operator_tables():
    derivative, lower, upper, back_lower, back_upper = lobatto_tables()
    eye = np.eye(4, dtype=np.float32)
    volume = np.concatenate(
        [
            np.kron(derivative, np.kron(eye, eye)),
            np.kron(eye, np.kron(derivative, eye)),
            np.kron(eye, np.kron(eye, derivative)),
        ],
        axis=1,
    )
    five = np.eye(5, dtype=np.float32)
    forward, backward = (lower, upper), (back_lower, back_upper)
    spread = np.concatenate(
        [np.kron(five, np.kron(forward[q % 2], forward[q // 2])) for q in range(4)], axis=0
    )
    gather = np.concatenate(
        [np.kron(five, np.kron(backward[q % 2], backward[q // 2])) for q in range(4)], axis=1
    )
    return volume, spread, gather


def split_table(table):
    kind = jnp.dtype(BF16)
    high = table.astype(kind)
    rest = table - high.astype(np.float32)
    middle = rest.astype(kind)
    return high, middle, (rest - middle.astype(np.float32)).astype(kind)


def read_lanes(state_hbm, lanes, sems):
    return [
        [
            pltpu.make_async_copy(
                state_hbm.at[var, :, pl.ds(block * LANES, LANES)],
                lanes.at[block, var],
                sems.at[block, var],
            )
            for var in range(5)
        ]
        for block in range(lanes.shape[0])
    ]


def face_part(lanes, block, var, face):
    if face < 2:
        return lanes[block, var, 48 * face : 48 * face + 16, :]
    if face < 4:
        start = 12 * (face % 2)
        return jnp.concatenate(
            [lanes[block, var, 16 * i + start : 16 * i + start + 4, :] for i in range(4)], axis=0
        )
    return lanes[block, var, pl.ds(3 * (face % 2), 16, stride=4), :]


def add_face(lanes, var, face, value, begin=0):
    for which in range(value.shape[1] // LANES):
        block = begin + which
        part = value[:, which * LANES : (which + 1) * LANES]
        if face < 2:
            lanes[block, var, 48 * face : 48 * face + 16, :] += part
        elif face < 4:
            start = 12 * (face % 2)
            for i in range(4):
                lanes[block, var, start + 16 * i : start + 16 * i + 4, :] += part[
                    4 * i : 4 * i + 4
                ]
        else:
            lanes[block, var, pl.ds(3 * (face % 2), 16, stride=4), :] += part


def three_pieces(value):
    high = value.astype(BF16)
    rest = value - high.astype(F32)
    middle = rest.astype(BF16)
    low = (rest - middle.astype(F32)).astype(BF16)
    return high, middle, low


def store_pieces(pieces, rows, columns, value):
    for which, piece in enumerate(three_pieces(value)):
        pieces[80 * which + rows : 80 * which + rows + value.shape[0], columns] = piece


ROWS = 512


def number_rows(grid):
    grid[...] = lax.broadcasted_iota(jnp.int32, grid.shape, 0).astype(jnp.int16)


def one_hot(grid, indices, count):
    width = indices.shape[1]
    rows = min(count, ROWS)
    row = jnp.broadcast_to(indices, (16, width)).astype(jnp.int16)
    spots = jnp.concatenate([grid[0:rows, :]] * (width // LANES), axis=1)
    parts = []
    for start in range(0, count, rows):
        want = jnp.concatenate([row - jnp.int16(start)] * (rows // 16), axis=0)
        parts.append(jnp.where(spots == want, jnp.ones((), BF16), jnp.zeros((), BF16)))
    return parts[0] if len(parts) == 1 else jnp.concatenate(parts, axis=0)


def split_product(table_ref, value):
    rows = table_ref.shape[0] // 3
    high, middle, low = three_pieces(value)
    first = jnp.dot(table_ref[...], high, preferred_element_type=F32)
    second = jnp.dot(table_ref[0 : 2 * rows, :], middle, preferred_element_type=F32)
    third = jnp.dot(table_ref[0:rows, :], low, preferred_element_type=F32)
    small = (first[2 * rows :] + second[rows:]) + third
    return first[0:rows] + ((first[rows : 2 * rows] + second[0:rows]) + small)


def joined(product):
    return (product[0:80] + product[80:160]) + product[160:240]


def primitives(cons):
    inverse = 1.0 / cons[0]
    motion = [cons[1 + axis] * inverse for axis in range(3)]
    pressure = (GAMMA - 1.0) * (
        cons[4] - 0.5 * (cons[1] * motion[0] + cons[2] * motion[1] + cons[3] * motion[2])
    )
    return inverse, motion, pressure


def axis_flux(cons, prim, axis, sign):
    _, motion, pressure = prim
    along = motion[axis] if sign > 0 else -motion[axis]
    push = pressure if sign > 0 else -pressure
    flux = [cons[v] * along for v in range(4)]
    flux[1 + axis] = flux[1 + axis] + push
    flux.append((cons[4] + pressure) * along)
    return flux


def sound(prim):
    inverse, _, pressure = prim
    return jnp.sqrt(GAMMA * pressure * inverse)


def normal_flux(cons, normal):
    inverse, motion, pressure = primitives(cons)
    along = motion[0] * normal[0] + motion[1] * normal[1] + motion[2] * normal[2]
    flux = [
        cons[0] * along,
        cons[1] * along + pressure * normal[0],
        cons[2] * along + pressure * normal[1],
        cons[3] * along + pressure * normal[2],
        (cons[4] + pressure) * along,
    ]
    return flux, jnp.abs(along) + jnp.sqrt(GAMMA * pressure * inverse)


def packed_places(count):
    return [0, count, 2 * count, LANES, LANES + count]


def highest(value):
    return jnp.max(value)


def send_kernel(hop, peers, *rest):
    inputs, outs, held = rest[:11], rest[11 : 11 + peers], rest[11 + peers : 21 + peers]
    traces, pieces, table, spots, grid, back_ref, sems, state_sems = rest[21 + peers :]
    lanes, faces_ref, mortar_ref, way_ref = held[:4]
    elems = inputs[0].shape[2]
    chunks = elems // LANES
    targets = [faces_ref, mortar_ref, way_ref, back_ref] + list(held[4:])
    loads = [
        pltpu.make_async_copy(source, target, sems.at[k])
        for k, (source, target) in enumerate(zip(inputs[1:], targets))
    ]
    copies = read_lanes(inputs[0], lanes, state_sems)
    for copy in loads[:4] + sum(copies, []) + loads[4:]:
        copy.start()
    slots = faces_ref.shape[1]
    count, backs = mortar_ref.shape[1], back_ref.shape[1]
    number_rows(grid)
    for copy in loads[:4]:
        copy.wait()

    wanted = [faces_ref[p : p + 1, :] for p in range(peers)]
    faces = faces_ref[...]
    face = sum((faces >= (k + 1) * elems).astype(jnp.int32) for k in range(6))
    least = jnp.min(jnp.where(face < 6, face, 5), axis=1, keepdims=True)
    most = jnp.max(jnp.where(face < 6, face, 0), axis=1, keepdims=True)
    longest = highest(most - least)
    starts = [least[p, 0] for p in range(peers)]
    stops = [most[p, 0] for p in range(peers)]

    table[...] = jnp.zeros(table.shape, F32)
    table[0:5, :] = mortar_ref[...].astype(F32)
    table[5:6, :] = way_ref[...].astype(F32)
    for side in range(2):
        for group in range(4):
            spots[side : side + 1, group * backs : (group + 1) * backs] = back_ref[
                side : side + 1, :
            ]
    lane = lax.broadcasted_iota(jnp.int32, (1, LANES), 1)
    group_of = sum((lane >= (k + 1) * backs).astype(jnp.int32) for k in range(3))
    empty = 6 * elems
    extra = []
    for side, target in ((0, 0), (1, hop)):
        entry = spots[side : side + 1, :]
        kind = sum((entry >= (k + 1) * count).astype(jnp.int32) for k in range(5))
        which = jnp.where(kind < 5, entry - kind * count, -1)
        rows = lax.broadcasted_iota(jnp.int32, (count, LANES), 0)
        found = jnp.dot(
            table[...],
            (rows == which).astype(F32),
            preferred_element_type=F32,
            precision=HIGHEST,
        )
        small = sum(jnp.where(group_of == k, found[1 + k : 2 + k], 0.0) for k in range(4))
        trace = jnp.where(kind == 0, small, found[0:1])
        unused = (kind == 5) | ((kind > 0) & (group_of > 0))
        trace = jnp.where(unused, float(empty), trace).astype(jnp.int32)
        slot = trace - (empty + 1) - (hop if side == 0 else 0) * slots
        code = jnp.where((trace > empty) & (slot >= 0) & (slot < slots), slot, -1)
        outs[target][80:88, slots:] = jnp.zeros((8, LANES), F32)
        outs[target][80:81, slots:] = code.astype(F32)
        outs[target][81:82, slots:] = kind.astype(F32)
        outs[target][82:83, slots:] = found[5:6]
        outs[target][80:88, 0:slots] = jnp.zeros((8, slots), F32)
        extra.append(trace)

    for block in range(chunks):
        for var in range(5):
            copies[block][var].wait()
        for var in range(5):
            rows = slice(16 * var, 16 * var + 16)
            for face in range(6):
                part = face_part(lanes, block, var, face)
                traces[face, rows, block * LANES : (block + 1) * LANES] = part
                if face < 4:
                    start = face * elems + block * LANES
                    store_pieces(pieces, 16 * var, slice(start, start + LANES), part)

    def collect(step, first):
        for p in range(peers):
            face = jnp.minimum(starts[p] + step, stops[p])
            local = wanted[p] - face * elems
            chunk_of = jnp.broadcast_to(lax.shift_right_arithmetic(local, 7), (8, LANES))
            spot = jnp.broadcast_to(jnp.bitwise_and(local, LANES - 1), (8, LANES))
            for r in range(10):
                rows = slice(8 * r, 8 * r + 8)
                value = jnp.zeros((8, LANES), F32) if first else outs[p][rows, 0:slots]
                for chunk in range(chunks):
                    part = traces[face, rows, chunk * LANES : (chunk + 1) * LANES]
                    value = jnp.where(
                        chunk_of == chunk, jnp.take_along_axis(part, spot, axis=1), value
                    )
                outs[p][rows, 0:slots] = value

    collect(0, True)
    product = jnp.dot(
        pieces[...],
        one_hot(grid, jnp.concatenate(extra, axis=1), 4 * elems),
        preferred_element_type=F32,
    )
    whole = joined(product)
    outs[0][0:80, slots:] = whole[:, 0:LANES]
    outs[hop][0:80, slots:] = whole[:, LANES:]

    @pl.loop(1, longest + 1)
    def _(step):
        collect(step, False)

    for copy in loads[4:]:
        copy.wait()


def local_kernel(
    lanes,
    partner_ref,
    mortar_ref,
    source_ref,
    level_ref,
    volume_ref,
    acc_ref,
    traces_ref,
    beside_ref,
    big_ref,
    own_ref,
    pieces,
    spots,
    grid,
):
    elems = partner_ref.shape[1]
    chunks = elems // LANES
    count = mortar_ref.shape[1]
    number_rows(grid)
    returned = own_ref.shape[1] // 2
    first_back = 5 * count + 1
    slot = lax.broadcasted_iota(jnp.int32, (returned, elems), 0) + first_back
    number = lax.broadcasted_iota(jnp.int32, (returned, elems), 1)
    hit = jnp.zeros((returned, elems), jnp.int32)
    for face in range(4):
        hit = jnp.where(source_ref[face : face + 1, :] == slot, number + (face * elems + 1), hit)
    column = jnp.sum(hit.astype(F32), axis=1, keepdims=True)
    corner = lax.broadcasted_iota(jnp.int32, (returned, LANES), 0) + count == (
        lax.broadcasted_iota(jnp.int32, (returned, LANES), 1)
    )
    owner = jnp.sum(jnp.where(corner, column, 0.0), axis=0, keepdims=True).astype(jnp.int32) - 1
    spots[...] = jnp.full(spots.shape, -1, jnp.int32)
    for row, place in enumerate(packed_places(count)):
        spots[0:1, place : place + count] = mortar_ref[row : row + 1, :]

    for face in range(6):
        for var in range(5):
            rows = slice(16 * var, 16 * var + 16)
            for block in range(chunks):
                part = face_part(lanes, block, var, face)
                columns = slice(
                    face * elems + block * LANES, face * elems + (block + 1) * LANES
                )
                traces_ref[rows, columns] = part
                if face < 4:
                    store_pieces(pieces, 16 * var, columns, part)

    def lane_gathered(wanted, first, last, out, column):
        spot = jnp.broadcast_to(jnp.bitwise_and(wanted, LANES - 1), (8, LANES))
        chunk_of = jnp.broadcast_to(lax.shift_right_arithmetic(wanted, 7), (8, LANES))
        for r in range(10):
            rows = slice(8 * r, 8 * r + 8)
            value = jnp.zeros((8, LANES), F32)
            for chunk in range(first, last):
                part = traces_ref[rows, chunk * LANES : (chunk + 1) * LANES]
                value = jnp.where(
                    chunk_of == chunk, jnp.take_along_axis(part, spot, axis=1), value
                )
            out[rows, column : column + LANES] = value

    def matrix_gathered(face):
        other = (face ^ 1) * elems
        product = jnp.dot(
            pieces[:, other : other + elems],
            one_hot(grid, partner_ref[face : face + 1, :] - other, elems),
            preferred_element_type=F32,
        )
        beside_ref[:, face * elems : (face + 1) * elems] = joined(product)

    wanted = spots[0:1, :]
    for face in range(4):
        matrix_gathered(face)
        if face < 2:
            for block in range(chunks):
                columns = slice(block * LANES, (block + 1) * LANES)
                first = ((4 + face) ^ 1) * chunks
                lane_gathered(
                    partner_ref[4 + face : 5 + face, columns],
                    first,
                    first + chunks,
                    beside_ref,
                    (4 + face) * elems + block * LANES,
                )
        if face == 2:
            lane_gathered(owner, 0, 4 * chunks, own_ref, 0)
    big_ref[...] = joined(
        jnp.dot(pieces[...], one_hot(grid, wanted, 4 * elems), preferred_element_type=F32)
    )
    factor = -(jnp.left_shift(2, level_ref[...]).astype(F32))
    cons = [
        jnp.concatenate([lanes[block, v] for block in range(chunks)], axis=1) for v in range(5)
    ]
    prim = primitives(cons)
    fluxes = [axis_flux(cons, prim, axis, 1) for axis in range(3)]
    for var in range(5):
        stacked = jnp.concatenate([fluxes[axis][var] for axis in range(3)], axis=0)
        total = factor * split_product(volume_ref, stacked)
        for block in range(chunks):
            acc_ref[block, var] = total[:, block * LANES : (block + 1) * LANES]


def with_reference(traces, empty):
    return jnp.concatenate(
        [
            jnp.where(empty, 1.0, traces[0:16]),
            jnp.where(empty, 0.0, traces[16:64]),
            jnp.where(empty, 2.5, traces[64:80]),
        ],
        axis=0,
    )


def finish_kernel(base, hop, peers, *rest):
    arrived = rest[:peers]
    (
        acc_ref,
        traces_ref,
        beside_ref,
        big_ref,
        own_ref,
        partner_ref,
        source_ref,
        faces_ref,
        mortar_ref,
        way_ref,
        level_ref,
        step_ref,
        spread_ref,
        gather_ref,
        out_hbm,
        sums,
        outside,
        pieces,
        fluxes,
        stars_of,
        payload,
        spots,
        grid,
        sems,
    ) = rest[peers:]
    slots = faces_ref.shape[1]
    elems = partner_ref.shape[1]
    chunks = elems // LANES
    count = mortar_ref.shape[1]
    empty = base - 1
    wide = 2 * slots
    backs = LANES // 4
    places = packed_places(count)

    number_rows(grid)
    whole_links = partner_ref[...]
    block_of = lax.shift_right_arithmetic(whole_links - base, wide.bit_length() - 1)
    least = jnp.min(jnp.where(block_of >= 0, block_of, peers // 2 - 1), axis=1, keepdims=True)
    most = jnp.max(block_of, axis=1, keepdims=True)
    starts = [least[face, 0] for face in range(6)]
    links = [partner_ref[face : face + 1, :] for face in range(6)]
    sources = [source_ref[face : face + 1, :] for face in range(4)]

    for peer in range(peers):
        for var in range(5):
            columns = slice((peer % 2) * slots, (peer % 2 + 1) * slots)
            for which, piece in enumerate(
                three_pieces(arrived[peer][16 * var : 16 * var + 16, 0:slots])
            ):
                row = 80 * which + 16 * var
                pieces[peer // 2, row : row + 16, columns] = piece
    payload[0] = arrived[0][:, slots:]
    payload[1] = arrived[hop][:, slots:]
    codes = [payload[side, 80:81, :] for side in range(2)]

    outside[...] = jnp.zeros(outside.shape, F32)
    split = jnp.maximum(highest(codes[0]), highest(codes[1])) >= 0.0

    @pl.when(split | (highest(most - least) > 0))
    def _():
        for face in range(6):

            @pl.loop(starts[face] + 1, most[face, 0] + 1)
            def _(block, face=face):
                outside[face] += joined(
                    jnp.dot(
                        pieces[block],
                        one_hot(grid, links[face] - base - block * wide, wide),
                        preferred_element_type=F32,
                    )
                )

        for side, row in ((0, hop), (1, 0)):
            code = codes[side].astype(jnp.int32)
            listed = jnp.take_along_axis(
                jnp.broadcast_to(faces_ref[row : row + 1, :], (8, LANES)),
                jnp.broadcast_to(jnp.maximum(code, 0), (8, LANES)),
                axis=1,
            )
            listed = jnp.where(jnp.broadcast_to(code, (8, LANES)) >= 0, listed, -1)
            chunk_of = lax.shift_right_arithmetic(listed, 7)
            spot = jnp.bitwise_and(listed, LANES - 1)
            for r in range(10):
                rows = slice(8 * r, 8 * r + 8)

                def pick(chunk, value):
                    start = pl.multiple_of(chunk * LANES, LANES)
                    part = traces_ref[rows, pl.ds(start, LANES)]
                    return jnp.where(
                        chunk_of == chunk, jnp.take_along_axis(part, spot, axis=1), value
                    )

                payload[side, rows, :] = lax.fori_loop(
                    0, 6 * chunks, pick, payload[side, rows, :]
                )

    factor = (-6.0 * step_ref[0]) * jnp.left_shift(2, level_ref[...]).astype(F32)
    sums[...] = step_ref[0] * acc_ref[...]

    def conform(face):
        axis, sign = face // 2, 2 * (face % 2) - 1
        columns = slice(face * elems, (face + 1) * elems)
        block = starts[face]
        near = joined(
            jnp.dot(
                pieces[block],
                one_hot(grid, links[face] - base - block * wide, wide),
                preferred_element_type=F32,
            )
        )
        near = near + (beside_ref[:, columns] + outside[face])
        first = [traces_ref[16 * v : 16 * v + 16, columns] for v in range(5)]
        second = [near[16 * v : 16 * v + 16, :] for v in range(5)]
        first_prim, second_prim = primitives(first), primitives(second)
        first_flux = axis_flux(first, first_prim, axis, sign)
        second_flux = axis_flux(second, second_prim, axis, sign)
        speed = jnp.maximum(
            jnp.abs(first_prim[1][axis]) + sound(first_prim),
            jnp.abs(second_prim[1][axis]) + sound(second_prim),
        )
        hanging = links[face] == empty
        for v in range(5):
            star = 0.5 * (second_flux[v] - first_flux[v]) - 0.5 * speed * (second[v] - first[v])
            jump = jnp.where(hanging, -first_flux[v], star)
            if face < 4:
                stars_of[face, 16 * v : 16 * v + 16, :] = jump
            else:
                add_face(sums, v, face, factor * jump)

    def mortar():
        spots[...] = jnp.full(spots.shape, empty, jnp.int32)
        for row, place in enumerate(places):
            spots[0:1, place : place + count] = mortar_ref[row : row + 1, :]
        spots[1:2, 0:count] = way_ref[...]
        packed = spots[0:1, :]
        total = jnp.zeros((240, wide), F32)
        for block in range(peers // 2):
            total = total + jnp.dot(
                pieces[block],
                one_hot(grid, packed - (base + block * wide), wide),
                preferred_element_type=F32,
            )
        both = joined(total) + big_ref[...]
        yield
        lane = lax.broadcasted_iota(jnp.int32, (1, LANES), 1)
        mine = lane < count
        backs_end = count + 2 * backs
        own = own_ref[...]
        moved = []
        for group in range(4):
            shift = group * backs
            parts = [
                pltpu.roll(payload[side], (count + side * backs - shift) % LANES, 1)
                for side in range(2)
            ]
            moved.append(jnp.where(lane < count + backs, parts[0], parts[1]))
        unused = (lane >= backs_end) | ((lane >= count) & (own[0:1] == 0.0))
        unused = unused | (mine & (packed[:, 0:LANES] == empty))
        kind = jnp.where(mine, 0, moved[0][81:82].astype(jnp.int32))
        way = jnp.where(mine, spots[1:2, 0:LANES], moved[0][82:83].astype(jnp.int32))
        large = kind == 0
        traces = []
        for row, place in enumerate(places):
            part = both[:, 0:LANES] if place < LANES else both[:, LANES:]
            shift = place % LANES
            part = part if shift == 0 else pltpu.roll(part, LANES - shift, 1)
            if row == 0:
                back = jnp.where(large, own, moved[0][0:80])
            else:
                back = jnp.where(large, moved[row - 1][0:80], own)
            traces.append(with_reference(jnp.where(mine, part, back), unused))
        normal = [
            (way == 2 * axis + 1).astype(F32) - (way == 2 * axis).astype(F32) for axis in range(3)
        ]
        near = split_product(spread_ref, traces[0])
        yield
        stars = []
        for quarter in range(4):
            first = [near[80 * quarter + 16 * v : 80 * quarter + 16 * v + 16] for v in range(5)]
            second = [traces[1 + quarter][16 * v : 16 * v + 16] for v in range(5)]
            first_flux, first_speed = normal_flux(first, normal)
            second_flux, second_speed = normal_flux(second, normal)
            speed = jnp.maximum(first_speed, second_speed)
            stars.append(
                jnp.concatenate(
                    [
                        0.5 * (first_flux[v] + second_flux[v])
                        - 0.5 * speed * (second[v] - first[v])
                        for v in range(5)
                    ],
                    axis=0,
                )
            )
            if quarter == 1:
                yield
        whole = split_product(gather_ref, jnp.concatenate(stars, axis=0))
        yield
        values = [whole] + [-star for star in stars]
        result = whole
        for quarter in range(4):
            result = jnp.where(kind == 1 + quarter, values[1 + quarter], result)
        halves = [jnp.zeros((80, LANES), F32), jnp.zeros((80, LANES), F32)]
        for row, place in enumerate(places):
            shift = place % LANES
            part = values[row] if shift == 0 else pltpu.roll(values[row], shift, 1)
            inside = (lane >= shift) & (lane < shift + count)
            halves[place // LANES] = jnp.where(inside, part, halves[place // LANES])
        for which, value in enumerate(halves + [result]):
            columns = slice(which * LANES, (which + 1) * LANES)
            for var in range(5):
                store_pieces(fluxes, 16 * var, columns, value[16 * var : 16 * var + 16])

    chain = mortar()
    for face in (4, 5, 0, 1, 2, 3):
        next(chain, None)
        conform(face)
    for _ in chain:
        pass

    columns = []
    for face in range(4):
        entry = sources[face]
        row = sum((entry >= (k + 1) * count).astype(jnp.int32) for k in range(4))
        spot = entry - row * count
        column = jnp.where(row >= 3, LANES + (row - 3) * count, row * count) + spot
        beyond = 2 * LANES + count + entry - (5 * count + 1)
        columns.append(
            jnp.where(entry < 5 * count, column, jnp.where(entry > 5 * count, beyond, -1))
        )
    copies = []
    span = 2 if chunks % 2 == 0 else 1
    for begin in range(0, chunks, span):
        part = slice(begin * LANES, (begin + span) * LANES)
        for face in range(4):
            star = joined(
                jnp.dot(
                    fluxes[...],
                    one_hot(grid, columns[face][:, part], 3 * LANES),
                    preferred_element_type=F32,
                )
            )
            for v in range(5):
                rows = slice(16 * v, 16 * v + 16)
                add_face(
                    sums, v, face, factor[:, part] * (stars_of[face, rows, part] + star[rows, :]), begin
                )
        for block in range(begin, begin + span):
            copy = pltpu.make_async_copy(
                sums.at[block], out_hbm.at[:, :, pl.ds(block * LANES, LANES)], sems.at[block]
            )
            copy.start()
            copies.append(copy)
    for copy in copies:
        copy.wait()


def body(
    state, step_size, levels, send_faces, partner, mortar_in, mortar_dir, return_faces, flux_source
):
    elems = state.shape[2]
    peers, slots = send_faces.shape
    hop = peers // 2
    count = mortar_dir.shape[0]
    base = 6 * elems + 1
    chunks = elems // LANES
    backs = return_faces.shape[1]
    if slots != LANES or 4 * backs != LANES or max(3 * count, count + 2 * backs) > LANES:
        raise ValueError("sizes")
    volume, spread, gather = (
        jnp.asarray(np.concatenate(split_table(t), axis=0)) for t in operator_tables()
    )
    way = mortar_dir.reshape(1, count)
    level = levels.reshape(1, elems)
    vmem = pl.BlockSpec(memory_space=pltpu.VMEM)
    smem = pl.BlockSpec(memory_space=pltpu.SMEM)
    hbm = pl.BlockSpec(memory_space=pltpu.HBM)
    lanes = jax.ShapeDtypeStruct((chunks, 5, 64, LANES), F32)
    sems = pltpu.SemaphoreType.DMA((chunks,))
    grid = pltpu.VMEM((ROWS, LANES), jnp.int16)

    shapes = [
        jax.ShapeDtypeStruct((88, 2 * slots) if p in (0, hop) else (80, slots), F32)
        for p in range(peers)
    ]
    inputs = [state, send_faces, mortar_in, way, return_faces, partner, flux_source, level]
    inputs += [volume, spread, gather]
    held = [lanes] + [
        jax.ShapeDtypeStruct(x.shape, x.dtype) for x in inputs[1:4] + inputs[5:]
    ]
    results = pl.pallas_call(
        functools.partial(send_kernel, hop, peers),
        out_shape=shapes + held,
        in_specs=[hbm] * len(inputs),
        out_specs=[vmem] * (peers + len(held)),
        scratch_shapes=[
            pltpu.VMEM((6, 80, elems), F32),
            pltpu.VMEM((240, 4 * elems), BF16),
            pltpu.VMEM((8, count), F32),
            pltpu.VMEM((8, LANES), jnp.int32),
            grid,
            pltpu.VMEM(return_faces.shape, jnp.int32),
            pltpu.SemaphoreType.DMA((len(inputs) - 1,)),
            pltpu.SemaphoreType.DMA((chunks, 5)),
        ],
        name="send",
        compiler_params=pltpu.CompilerParams(vmem_limit_bytes=14 << 20),
    )(*[pltpu.with_memory_space_constraint(x, pltpu.HBM) for x in inputs])
    outgoing = results[:peers]
    state, send_faces, mortar_in, way, partner, flux_source, level = results[peers : peers + 7]
    volume, spread, gather = results[peers + 7 :]
    arrived = []
    for peer in range(peers):
        distance = peer + 1 if peer < hop else hop - 1 - peer
        arrived.append(passed_along(outgoing[peer], "dev", distance))
    acc, traces, beside, big, own = pl.pallas_call(
        local_kernel,
        out_shape=[
            lanes,
            jax.ShapeDtypeStruct((80, 6 * elems), F32),
            jax.ShapeDtypeStruct((80, 6 * elems), F32),
            jax.ShapeDtypeStruct((80, 2 * LANES), F32),
            jax.ShapeDtypeStruct((80, LANES), F32),
        ],
        in_specs=[vmem] * 6,
        out_specs=[vmem] * 5,
        scratch_shapes=[
            pltpu.VMEM((240, 4 * elems), BF16),
            pltpu.VMEM((8, 2 * LANES), jnp.int32),
            grid,
        ],
        name="local",
        compiler_params=pltpu.CompilerParams(vmem_limit_bytes=14 << 20),
    )(state, partner, mortar_in, flux_source, level, volume)
    return pl.pallas_call(
        functools.partial(finish_kernel, base, hop, peers),
        out_shape=jax.ShapeDtypeStruct((5, 64, elems), F32),
        in_specs=[vmem] * (peers + 11) + [smem, vmem, vmem],
        out_specs=hbm,
        scratch_shapes=[
            pltpu.VMEM(lanes.shape, F32),
            pltpu.VMEM((6, 80, elems), F32),
            pltpu.VMEM((peers // 2, 240, 2 * slots), BF16),
            pltpu.VMEM((240, 3 * LANES), BF16),
            pltpu.VMEM((4, 80, elems), F32),
            pltpu.VMEM((2, 88, LANES), F32),
            pltpu.VMEM((8, 2 * LANES), jnp.int32),
            grid,
            sems,
        ],
        name="finish",
        compiler_params=pltpu.CompilerParams(vmem_limit_bytes=14 << 20),
    )(
        *arrived,
        acc,
        traces,
        beside,
        big,
        own,
        partner,
        flux_source,
        send_faces,
        mortar_in,
        way,
        level,
        step_size,
        spread,
        gather,
    )


def solution(mesh):
    placed = (
        P(None, None, "dev"),
        P(),
        P("dev"),
        P("dev", None),
        P(None, "dev"),
        P(None, "dev"),
        P("dev"),
        P("dev", None),
        P(None, "dev"),
    )

    return jax.shard_map(
        body, mesh=mesh, in_specs=placed, out_specs=P(None, None, "dev"), check_vma=False
    )
```

```python
import functools

import jax
import jax.numpy as jnp
import numpy as np
from jax import lax
from jax.experimental import pallas as pl
from jax.experimental.pallas import tpu as pltpu
from jax.sharding import PartitionSpec as P


GAMMA = 1.4
HIGHEST = lax.Precision.HIGHEST
F32 = jnp.float32
BF16 = jnp.bfloat16
LANES = 128


def passed_along(block, axis, distance):
    devices = range(lax.axis_size(axis))
    route = [((i - distance) % len(devices), i) for i in devices]
    return lax.ppermute(block, axis, route)


def lobatto_tables():
    nodes = np.array([-1.0, -1.0 / np.sqrt(5.0), 1.0 / np.sqrt(5.0), 1.0])
    weights = np.array([1.0, 5.0, 5.0, 1.0]) / 6.0

    def basis(points):
        table = np.ones((len(points), 4))
        for column in range(4):
            for other in range(4):
                if other != column:
                    table[:, column] *= (points - nodes[other]) / (nodes[column] - nodes[other])
        return table

    derivative = np.zeros((4, 4))
    for row in range(4):
        for column in range(4):
            total = 0.0
            for other in range(4):
                if other != column:
                    term = 1.0 / (nodes[column] - nodes[other])
                    for third in range(4):
                        if third != column and third != other:
                            term *= (nodes[row] - nodes[third]) / (nodes[column] - nodes[third])
                    total += term
            derivative[row, column] = total
    lower = basis((nodes - 1.0) / 2.0)
    upper = basis((nodes + 1.0) / 2.0)
    back_lower = 0.5 * (lower.T * weights[None, :]) / weights[:, None]
    back_upper = 0.5 * (upper.T * weights[None, :]) / weights[:, None]
    return [
        np.asarray(table, np.float32)
        for table in (derivative, lower, upper, back_lower, back_upper)
    ]


def operator_tables():
    derivative, lower, upper, back_lower, back_upper = lobatto_tables()
    eye = np.eye(4, dtype=np.float32)
    volume = np.concatenate(
        [
            np.kron(derivative, np.kron(eye, eye)),
            np.kron(eye, np.kron(derivative, eye)),
            np.kron(eye, np.kron(eye, derivative)),
        ],
        axis=1,
    )
    five = np.eye(5, dtype=np.float32)
    forward, backward = (lower, upper), (back_lower, back_upper)
    spread = np.concatenate(
        [np.kron(five, np.kron(forward[q % 2], forward[q // 2])) for q in range(4)], axis=0
    )
    gather = np.concatenate(
        [np.kron(five, np.kron(backward[q % 2], backward[q // 2])) for q in range(4)], axis=1
    )
    return volume, spread, gather


def split_table(table):
    kind = jnp.dtype(BF16)
    high = table.astype(kind)
    rest = table - high.astype(np.float32)
    middle = rest.astype(kind)
    return high, middle, (rest - middle.astype(np.float32)).astype(kind)


def read_lanes(state_hbm, lanes, sems):
    return [
        [
            pltpu.make_async_copy(
                state_hbm.at[var, :, pl.ds(block * LANES, LANES)],
                lanes.at[block, var],
                sems.at[block, var],
            )
            for var in range(5)
        ]
        for block in range(lanes.shape[0])
    ]


def face_part(lanes, block, var, face):
    if face < 2:
        return lanes[block, var, 48 * face : 48 * face + 16, :]
    if face < 4:
        start = 12 * (face % 2)
        return jnp.concatenate(
            [lanes[block, var, 16 * i + start : 16 * i + start + 4, :] for i in range(4)], axis=0
        )
    return lanes[block, var, pl.ds(3 * (face % 2), 16, stride=4), :]


def add_face(lanes, var, face, value, begin=0):
    for which in range(value.shape[1] // LANES):
        block = begin + which
        part = value[:, which * LANES : (which + 1) * LANES]
        if face < 2:
            lanes[block, var, 48 * face : 48 * face + 16, :] += part
        elif face < 4:
            start = 12 * (face % 2)
            for i in range(4):
                lanes[block, var, start + 16 * i : start + 16 * i + 4, :] += part[
                    4 * i : 4 * i + 4
                ]
        else:
            lanes[block, var, pl.ds(3 * (face % 2), 16, stride=4), :] += part


def three_pieces(value):
    high = value.astype(BF16)
    rest = value - high.astype(F32)
    middle = rest.astype(BF16)
    low = (rest - middle.astype(F32)).astype(BF16)
    return high, middle, low


def store_pieces(pieces, rows, columns, value):
    for which, piece in enumerate(three_pieces(value)):
        pieces[80 * which + rows : 80 * which + rows + value.shape[0], columns] = piece


ROWS = 512


def number_rows(grid):
    grid[...] = lax.broadcasted_iota(jnp.int32, grid.shape, 0).astype(jnp.int16)


def one_hot(grid, indices, count):
    width = indices.shape[1]
    rows = min(count, ROWS)
    row = jnp.broadcast_to(indices, (16, width)).astype(jnp.int16)
    spots = jnp.concatenate([grid[0:rows, :]] * (width // LANES), axis=1)
    parts = []
    for start in range(0, count, rows):
        want = jnp.concatenate([row - jnp.int16(start)] * (rows // 16), axis=0)
        parts.append(jnp.where(spots == want, jnp.ones((), BF16), jnp.zeros((), BF16)))
    return parts[0] if len(parts) == 1 else jnp.concatenate(parts, axis=0)


def split_product(table_ref, value):
    rows = table_ref.shape[0] // 3
    high, middle, low = three_pieces(value)
    first = jnp.dot(table_ref[...], high, preferred_element_type=F32)
    second = jnp.dot(table_ref[0 : 2 * rows, :], middle, preferred_element_type=F32)
    third = jnp.dot(table_ref[0:rows, :], low, preferred_element_type=F32)
    small = (first[2 * rows :] + second[rows:]) + third
    return first[0:rows] + ((first[rows : 2 * rows] + second[0:rows]) + small)


def joined(product):
    return (product[0:80] + product[80:160]) + product[160:240]


def primitives(cons):
    inverse = 1.0 / cons[0]
    motion = [cons[1 + axis] * inverse for axis in range(3)]
    pressure = (GAMMA - 1.0) * (
        cons[4] - 0.5 * (cons[1] * motion[0] + cons[2] * motion[1] + cons[3] * motion[2])
    )
    return inverse, motion, pressure


def axis_flux(cons, prim, axis, sign):
    _, motion, pressure = prim
    along = motion[axis] if sign > 0 else -motion[axis]
    push = pressure if sign > 0 else -pressure
    flux = [cons[v] * along for v in range(4)]
    flux[1 + axis] = flux[1 + axis] + push
    flux.append((cons[4] + pressure) * along)
    return flux


def sound(prim):
    inverse, _, pressure = prim
    return jnp.sqrt(GAMMA * pressure * inverse)


def normal_flux(cons, normal):
    inverse, motion, pressure = primitives(cons)
    along = motion[0] * normal[0] + motion[1] * normal[1] + motion[2] * normal[2]
    flux = [
        cons[0] * along,
        cons[1] * along + pressure * normal[0],
        cons[2] * along + pressure * normal[1],
        cons[3] * along + pressure * normal[2],
        (cons[4] + pressure) * along,
    ]
    return flux, jnp.abs(along) + jnp.sqrt(GAMMA * pressure * inverse)


def packed_places(count):
    return [0, count, 2 * count, LANES, LANES + count]


def highest(value):
    return jnp.max(value)


def send_kernel(hop, peers, *rest):
    inputs, outs, held = rest[:11], rest[11 : 11 + peers], rest[11 + peers : 21 + peers]
    traces, pieces, table, spots, grid, back_ref, sems, state_sems = rest[21 + peers :]
    lanes, faces_ref, mortar_ref, way_ref = held[:4]
    elems = inputs[0].shape[2]
    chunks = elems // LANES
    targets = [faces_ref, mortar_ref, way_ref, back_ref] + list(held[4:])
    loads = [
        pltpu.make_async_copy(source, target, sems.at[k])
        for k, (source, target) in enumerate(zip(inputs[1:], targets))
    ]
    copies = read_lanes(inputs[0], lanes, state_sems)
    for copy in loads[:4] + sum(copies, []) + loads[4:]:
        copy.start()
    slots = faces_ref.shape[1]
    count, backs = mortar_ref.shape[1], back_ref.shape[1]
    number_rows(grid)
    for copy in loads[:4]:
        copy.wait()

    wanted = [faces_ref[p : p + 1, :] for p in range(peers)]
    faces = faces_ref[...]
    face = sum((faces >= (k + 1) * elems).astype(jnp.int32) for k in range(6))
    least = jnp.min(jnp.where(face < 6, face, 5), axis=1, keepdims=True)
    most = jnp.max(jnp.where(face < 6, face, 0), axis=1, keepdims=True)
    longest = highest(most - least)
    starts = [least[p, 0] for p in range(peers)]
    stops = [most[p, 0] for p in range(peers)]

    table[...] = jnp.zeros(table.shape, F32)
    table[0:5, :] = mortar_ref[...].astype(F32)
    table[5:6, :] = way_ref[...].astype(F32)
    for side in range(2):
        for group in range(4):
            spots[side : side + 1, group * backs : (group + 1) * backs] = back_ref[
                side : side + 1, :
            ]
    lane = lax.broadcasted_iota(jnp.int32, (1, LANES), 1)
    group_of = sum((lane >= (k + 1) * backs).astype(jnp.int32) for k in range(3))
    empty = 6 * elems
    extra = []
    for side, target in ((0, 0), (1, hop)):
        entry = spots[side : side + 1, :]
        kind = sum((entry >= (k + 1) * count).astype(jnp.int32) for k in range(5))
        which = jnp.where(kind < 5, entry - kind * count, -1)
        rows = lax.broadcasted_iota(jnp.int32, (count, LANES), 0)
        found = jnp.dot(
            table[...],
            (rows == which).astype(F32),
            preferred_element_type=F32,
            precision=HIGHEST,
        )
        small = sum(jnp.where(group_of == k, found[1 + k : 2 + k], 0.0) for k in range(4))
        trace = jnp.where(kind == 0, small, found[0:1])
        unused = (kind == 5) | ((kind > 0) & (group_of > 0))
        trace = jnp.where(unused, float(empty), trace).astype(jnp.int32)
        slot = trace - (empty + 1) - (hop if side == 0 else 0) * slots
        code = jnp.where((trace > empty) & (slot >= 0) & (slot < slots), slot, -1)
        outs[target][80:88, slots:] = jnp.zeros((8, LANES), F32)
        outs[target][80:81, slots:] = code.astype(F32)
        outs[target][81:82, slots:] = kind.astype(F32)
        outs[target][82:83, slots:] = found[5:6]
        outs[target][80:88, 0:slots] = jnp.zeros((8, slots), F32)
        extra.append(trace)

    for block in range(chunks):
        for var in range(5):
            copies[block][var].wait()
        for var in range(5):
            rows = slice(16 * var, 16 * var + 16)
            for face in range(6):
                part = face_part(lanes, block, var, face)
                traces[face, rows, block * LANES : (block + 1) * LANES] = part
                if face < 4:
                    start = face * elems + block * LANES
                    store_pieces(pieces, 16 * var, slice(start, start + LANES), part)

    def collect(step, first):
        for p in range(peers):
            face = jnp.minimum(starts[p] + step, stops[p])
            local = wanted[p] - face * elems
            chunk_of = jnp.broadcast_to(lax.shift_right_arithmetic(local, 7), (8, LANES))
            spot = jnp.broadcast_to(jnp.bitwise_and(local, LANES - 1), (8, LANES))
            for r in range(10):
                rows = slice(8 * r, 8 * r + 8)
                value = jnp.zeros((8, LANES), F32) if first else outs[p][rows, 0:slots]
                for chunk in range(chunks):
                    part = traces[face, rows, chunk * LANES : (chunk + 1) * LANES]
                    value = jnp.where(
                        chunk_of == chunk, jnp.take_along_axis(part, spot, axis=1), value
                    )
                outs[p][rows, 0:slots] = value

    collect(0, True)
    product = jnp.dot(
        pieces[...],
        one_hot(grid, jnp.concatenate(extra, axis=1), 4 * elems),
        preferred_element_type=F32,
    )
    whole = joined(product)
    outs[0][0:80, slots:] = whole[:, 0:LANES]
    outs[hop][0:80, slots:] = whole[:, LANES:]

    @pl.loop(1, longest + 1)
    def _(step):
        collect(step, False)

    for copy in loads[4:]:
        copy.wait()


def local_kernel(
    lanes,
    partner_ref,
    mortar_ref,
    source_ref,
    level_ref,
    volume_ref,
    acc_ref,
    traces_ref,
    beside_ref,
    big_ref,
    own_ref,
    pieces,
    spots,
    grid,
):
    elems = partner_ref.shape[1]
    chunks = elems // LANES
    count = mortar_ref.shape[1]
    number_rows(grid)
    returned = own_ref.shape[1] // 2
    first_back = 5 * count + 1
    slot = lax.broadcasted_iota(jnp.int32, (returned, elems), 0) + first_back
    number = lax.broadcasted_iota(jnp.int32, (returned, elems), 1)
    hit = jnp.zeros((returned, elems), jnp.int32)
    for face in range(4):
        hit = jnp.where(source_ref[face : face + 1, :] == slot, number + (face * elems + 1), hit)
    column = jnp.sum(hit.astype(F32), axis=1, keepdims=True)
    corner = lax.broadcasted_iota(jnp.int32, (returned, LANES), 0) + count == (
        lax.broadcasted_iota(jnp.int32, (returned, LANES), 1)
    )
    owner = jnp.sum(jnp.where(corner, column, 0.0), axis=0, keepdims=True).astype(jnp.int32) - 1
    spots[...] = jnp.full(spots.shape, -1, jnp.int32)
    for row, place in enumerate(packed_places(count)):
        spots[0:1, place : place + count] = mortar_ref[row : row + 1, :]

    for face in range(6):
        for var in range(5):
            rows = slice(16 * var, 16 * var + 16)
            for block in range(chunks):
                part = face_part(lanes, block, var, face)
                columns = slice(
                    face * elems + block * LANES, face * elems + (block + 1) * LANES
                )
                traces_ref[rows, columns] = part
                if face < 4:
                    store_pieces(pieces, 16 * var, columns, part)

    def lane_gathered(wanted, first, last, out, column):
        spot = jnp.broadcast_to(jnp.bitwise_and(wanted, LANES - 1), (8, LANES))
        chunk_of = jnp.broadcast_to(lax.shift_right_arithmetic(wanted, 7), (8, LANES))
        for r in range(10):
            rows = slice(8 * r, 8 * r + 8)
            value = jnp.zeros((8, LANES), F32)
            for chunk in range(first, last):
                part = traces_ref[rows, chunk * LANES : (chunk + 1) * LANES]
                value = jnp.where(
                    chunk_of == chunk, jnp.take_along_axis(part, spot, axis=1), value
                )
            out[rows, column : column + LANES] = value

    def matrix_gathered(face):
        other = (face ^ 1) * elems
        product = jnp.dot(
            pieces[:, other : other + elems],
            one_hot(grid, partner_ref[face : face + 1, :] - other, elems),
            preferred_element_type=F32,
        )
        beside_ref[:, face * elems : (face + 1) * elems] = joined(product)

    wanted = spots[0:1, :]
    for face in range(4):
        matrix_gathered(face)
        if face < 2:
            for block in range(chunks):
                columns = slice(block * LANES, (block + 1) * LANES)
                first = ((4 + face) ^ 1) * chunks
                lane_gathered(
                    partner_ref[4 + face : 5 + face, columns],
                    first,
                    first + chunks,
                    beside_ref,
                    (4 + face) * elems + block * LANES,
                )
        if face == 2:
            lane_gathered(owner, 0, 4 * chunks, own_ref, 0)
    big_ref[...] = joined(
        jnp.dot(pieces[...], one_hot(grid, wanted, 4 * elems), preferred_element_type=F32)
    )
    factor = -(jnp.left_shift(2, level_ref[...]).astype(F32))
    cons = [
        jnp.concatenate([lanes[block, v] for block in range(chunks)], axis=1) for v in range(5)
    ]
    prim = primitives(cons)
    fluxes = [axis_flux(cons, prim, axis, 1) for axis in range(3)]
    for var in range(5):
        stacked = jnp.concatenate([fluxes[axis][var] for axis in range(3)], axis=0)
        total = factor * split_product(volume_ref, stacked)
        for block in range(chunks):
            acc_ref[block, var] = total[:, block * LANES : (block + 1) * LANES]


def early_kernel(hop, *refs):
    @pl.when(lax.axis_index("dev") < hop)
    def _():
        local_kernel(*refs)


def late_kernel(hop, *refs):
    inputs, earlier, rest = refs[:6], refs[6:11], refs[11:]
    ahead = lax.axis_index("dev") < hop

    @pl.when(ahead)
    def _():
        for source, target in zip(earlier, rest[:5]):
            target[...] = source[...]

    @pl.when(jnp.logical_not(ahead))
    def _():
        local_kernel(*inputs, *rest)


def with_reference(traces, empty):
    return jnp.concatenate(
        [
            jnp.where(empty, 1.0, traces[0:16]),
            jnp.where(empty, 0.0, traces[16:64]),
            jnp.where(empty, 2.5, traces[64:80]),
        ],
        axis=0,
    )


def finish_kernel(base, hop, peers, *rest):
    arrived = rest[:peers]
    (
        acc_ref,
        traces_ref,
        beside_ref,
        big_ref,
        own_ref,
        partner_ref,
        source_ref,
        faces_ref,
        mortar_ref,
        way_ref,
        level_ref,
        step_ref,
        spread_ref,
        gather_ref,
        out_hbm,
        sums,
        outside,
        pieces,
        fluxes,
        stars_of,
        payload,
        spots,
        grid,
        sems,
    ) = rest[peers:]
    slots = faces_ref.shape[1]
    elems = partner_ref.shape[1]
    chunks = elems // LANES
    count = mortar_ref.shape[1]
    empty = base - 1
    wide = 2 * slots
    backs = LANES // 4
    places = packed_places(count)

    number_rows(grid)
    whole_links = partner_ref[...]
    block_of = lax.shift_right_arithmetic(whole_links - base, wide.bit_length() - 1)
    least = jnp.min(jnp.where(block_of >= 0, block_of, peers // 2 - 1), axis=1, keepdims=True)
    most = jnp.max(block_of, axis=1, keepdims=True)
    starts = [least[face, 0] for face in range(6)]
    links = [partner_ref[face : face + 1, :] for face in range(6)]
    sources = [source_ref[face : face + 1, :] for face in range(4)]

    for peer in range(peers):
        for var in range(5):
            columns = slice((peer % 2) * slots, (peer % 2 + 1) * slots)
            for which, piece in enumerate(
                three_pieces(arrived[peer][16 * var : 16 * var + 16, 0:slots])
            ):
                row = 80 * which + 16 * var
                pieces[peer // 2, row : row + 16, columns] = piece
    payload[0] = arrived[0][:, slots:]
    payload[1] = arrived[hop][:, slots:]
    codes = [payload[side, 80:81, :] for side in range(2)]

    outside[...] = jnp.zeros(outside.shape, F32)
    split = jnp.maximum(highest(codes[0]), highest(codes[1])) >= 0.0

    @pl.when(split | (highest(most - least) > 0))
    def _():
        for face in range(6):

            @pl.loop(starts[face] + 1, most[face, 0] + 1)
            def _(block, face=face):
                outside[face] += joined(
                    jnp.dot(
                        pieces[block],
                        one_hot(grid, links[face] - base - block * wide, wide),
                        preferred_element_type=F32,
                    )
                )

        for side, row in ((0, hop), (1, 0)):
            code = codes[side].astype(jnp.int32)
            listed = jnp.take_along_axis(
                jnp.broadcast_to(faces_ref[row : row + 1, :], (8, LANES)),
                jnp.broadcast_to(jnp.maximum(code, 0), (8, LANES)),
                axis=1,
            )
            listed = jnp.where(jnp.broadcast_to(code, (8, LANES)) >= 0, listed, -1)
            chunk_of = lax.shift_right_arithmetic(listed, 7)
            spot = jnp.bitwise_and(listed, LANES - 1)
            for r in range(10):
                rows = slice(8 * r, 8 * r + 8)

                def pick(chunk, value):
                    start = pl.multiple_of(chunk * LANES, LANES)
                    part = traces_ref[rows, pl.ds(start, LANES)]
                    return jnp.where(
                        chunk_of == chunk, jnp.take_along_axis(part, spot, axis=1), value
                    )

                payload[side, rows, :] = lax.fori_loop(
                    0, 6 * chunks, pick, payload[side, rows, :]
                )

    factor = (-6.0 * step_ref[0]) * jnp.left_shift(2, level_ref[...]).astype(F32)
    sums[...] = step_ref[0] * acc_ref[...]

    def conform(face):
        axis, sign = face // 2, 2 * (face % 2) - 1
        columns = slice(face * elems, (face + 1) * elems)
        block = starts[face]
        near = joined(
            jnp.dot(
                pieces[block],
                one_hot(grid, links[face] - base - block * wide, wide),
                preferred_element_type=F32,
            )
        )
        near = near + (beside_ref[:, columns] + outside[face])
        first = [traces_ref[16 * v : 16 * v + 16, columns] for v in range(5)]
        second = [near[16 * v : 16 * v + 16, :] for v in range(5)]
        first_prim, second_prim = primitives(first), primitives(second)
        first_flux = axis_flux(first, first_prim, axis, sign)
        second_flux = axis_flux(second, second_prim, axis, sign)
        speed = jnp.maximum(
            jnp.abs(first_prim[1][axis]) + sound(first_prim),
            jnp.abs(second_prim[1][axis]) + sound(second_prim),
        )
        hanging = links[face] == empty
        for v in range(5):
            star = 0.5 * (second_flux[v] - first_flux[v]) - 0.5 * speed * (second[v] - first[v])
            jump = jnp.where(hanging, -first_flux[v], star)
            if face < 4:
                stars_of[face, 16 * v : 16 * v + 16, :] = jump
            else:
                add_face(sums, v, face, factor * jump)

    def mortar():
        spots[...] = jnp.full(spots.shape, empty, jnp.int32)
        for row, place in enumerate(places):
            spots[0:1, place : place + count] = mortar_ref[row : row + 1, :]
        spots[1:2, 0:count] = way_ref[...]
        packed = spots[0:1, :]
        total = jnp.zeros((240, wide), F32)
        for block in range(peers // 2):
            total = total + jnp.dot(
                pieces[block],
                one_hot(grid, packed - (base + block * wide), wide),
                preferred_element_type=F32,
            )
        both = joined(total) + big_ref[...]
        yield
        lane = lax.broadcasted_iota(jnp.int32, (1, LANES), 1)
        mine = lane < count
        backs_end = count + 2 * backs
        own = own_ref[...]
        moved = []
        for group in range(4):
            shift = group * backs
            parts = [
                pltpu.roll(payload[side], (count + side * backs - shift) % LANES, 1)
                for side in range(2)
            ]
            moved.append(jnp.where(lane < count + backs, parts[0], parts[1]))
        unused = (lane >= backs_end) | ((lane >= count) & (own[0:1] == 0.0))
        unused = unused | (mine & (packed[:, 0:LANES] == empty))
        kind = jnp.where(mine, 0, moved[0][81:82].astype(jnp.int32))
        way = jnp.where(mine, spots[1:2, 0:LANES], moved[0][82:83].astype(jnp.int32))
        large = kind == 0
        traces = []
        for row, place in enumerate(places):
            part = both[:, 0:LANES] if place < LANES else both[:, LANES:]
            shift = place % LANES
            part = part if shift == 0 else pltpu.roll(part, LANES - shift, 1)
            if row == 0:
                back = jnp.where(large, own, moved[0][0:80])
            else:
                back = jnp.where(large, moved[row - 1][0:80], own)
            traces.append(with_reference(jnp.where(mine, part, back), unused))
        normal = [
            (way == 2 * axis + 1).astype(F32) - (way == 2 * axis).astype(F32) for axis in range(3)
        ]
        near = split_product(spread_ref, traces[0])
        yield
        stars = []
        for quarter in range(4):
            first = [near[80 * quarter + 16 * v : 80 * quarter + 16 * v + 16] for v in range(5)]
            second = [traces[1 + quarter][16 * v : 16 * v + 16] for v in range(5)]
            first_flux, first_speed = normal_flux(first, normal)
            second_flux, second_speed = normal_flux(second, normal)
            speed = jnp.maximum(first_speed, second_speed)
            stars.append(
                jnp.concatenate(
                    [
                        0.5 * (first_flux[v] + second_flux[v])
                        - 0.5 * speed * (second[v] - first[v])
                        for v in range(5)
                    ],
                    axis=0,
                )
            )
            if quarter == 1:
                yield
        whole = split_product(gather_ref, jnp.concatenate(stars, axis=0))
        yield
        values = [whole] + [-star for star in stars]
        result = whole
        for quarter in range(4):
            result = jnp.where(kind == 1 + quarter, values[1 + quarter], result)
        halves = [jnp.zeros((80, LANES), F32), jnp.zeros((80, LANES), F32)]
        for row, place in enumerate(places):
            shift = place % LANES
            part = values[row] if shift == 0 else pltpu.roll(values[row], shift, 1)
            inside = (lane >= shift) & (lane < shift + count)
            halves[place // LANES] = jnp.where(inside, part, halves[place // LANES])
        for which, value in enumerate(halves + [result]):
            columns = slice(which * LANES, (which + 1) * LANES)
            for var in range(5):
                store_pieces(fluxes, 16 * var, columns, value[16 * var : 16 * var + 16])

    chain = mortar()
    for face in (4, 5, 0, 1, 2, 3):
        next(chain, None)
        conform(face)
    for _ in chain:
        pass

    columns = []
    for face in range(4):
        entry = sources[face]
        row = sum((entry >= (k + 1) * count).astype(jnp.int32) for k in range(4))
        spot = entry - row * count
        column = jnp.where(row >= 3, LANES + (row - 3) * count, row * count) + spot
        beyond = 2 * LANES + count + entry - (5 * count + 1)
        columns.append(
            jnp.where(entry < 5 * count, column, jnp.where(entry > 5 * count, beyond, -1))
        )
    copies = []
    span = 2 if chunks % 2 == 0 else 1
    for begin in range(0, chunks, span):
        part = slice(begin * LANES, (begin + span) * LANES)
        for face in range(4):
            star = joined(
                jnp.dot(
                    fluxes[...],
                    one_hot(grid, columns[face][:, part], 3 * LANES),
                    preferred_element_type=F32,
                )
            )
            for v in range(5):
                rows = slice(16 * v, 16 * v + 16)
                add_face(
                    sums, v, face, factor[:, part] * (stars_of[face, rows, part] + star[rows, :]), begin
                )
        for block in range(begin, begin + span):
            copy = pltpu.make_async_copy(
                sums.at[block], out_hbm.at[:, :, pl.ds(block * LANES, LANES)], sems.at[block]
            )
            copy.start()
            copies.append(copy)
    for copy in copies:
        copy.wait()


def body(
    state, step_size, levels, send_faces, partner, mortar_in, mortar_dir, return_faces, flux_source
):
    elems = state.shape[2]
    peers, slots = send_faces.shape
    hop = peers // 2
    count = mortar_dir.shape[0]
    base = 6 * elems + 1
    chunks = elems // LANES
    backs = return_faces.shape[1]
    if slots != LANES or 4 * backs != LANES or max(3 * count, count + 2 * backs) > LANES:
        raise ValueError("sizes")
    volume, spread, gather = (
        jnp.asarray(np.concatenate(split_table(t), axis=0)) for t in operator_tables()
    )
    way = mortar_dir.reshape(1, count)
    level = levels.reshape(1, elems)
    vmem = pl.BlockSpec(memory_space=pltpu.VMEM)
    smem = pl.BlockSpec(memory_space=pltpu.SMEM)
    hbm = pl.BlockSpec(memory_space=pltpu.HBM)
    lanes = jax.ShapeDtypeStruct((chunks, 5, 64, LANES), F32)
    sems = pltpu.SemaphoreType.DMA((chunks,))
    grid = pltpu.VMEM((ROWS, LANES), jnp.int16)

    shapes = [
        jax.ShapeDtypeStruct((88, 2 * slots) if p in (0, hop) else (80, slots), F32)
        for p in range(peers)
    ]
    inputs = [state, send_faces, mortar_in, way, return_faces, partner, flux_source, level]
    inputs += [volume, spread, gather]
    held = [lanes] + [
        jax.ShapeDtypeStruct(x.shape, x.dtype) for x in inputs[1:4] + inputs[5:]
    ]
    results = pl.pallas_call(
        functools.partial(send_kernel, hop, peers),
        out_shape=shapes + held,
        in_specs=[hbm] * len(inputs),
        out_specs=[vmem] * (peers + len(held)),
        scratch_shapes=[
            pltpu.VMEM((6, 80, elems), F32),
            pltpu.VMEM((240, 4 * elems), BF16),
            pltpu.VMEM((8, count), F32),
            pltpu.VMEM((8, LANES), jnp.int32),
            grid,
            pltpu.VMEM(return_faces.shape, jnp.int32),
            pltpu.SemaphoreType.DMA((len(inputs) - 1,)),
            pltpu.SemaphoreType.DMA((chunks, 5)),
        ],
        name="send",
        compiler_params=pltpu.CompilerParams(vmem_limit_bytes=14 << 20),
    )(*[pltpu.with_memory_space_constraint(x, pltpu.HBM) for x in inputs])
    outgoing = results[:peers]
    state, send_faces, mortar_in, way, partner, flux_source, level = results[peers : peers + 7]
    volume, spread, gather = results[peers + 7 :]
    arrived = []
    for peer in range(peers):
        distance = peer + 1 if peer < hop else hop - 1 - peer
        arrived.append(passed_along(outgoing[peer], "dev", distance))
    inputs = (state, partner, mortar_in, flux_source, level, volume)
    common = dict(
        out_shape=[
            lanes,
            jax.ShapeDtypeStruct((80, 6 * elems), F32),
            jax.ShapeDtypeStruct((80, 6 * elems), F32),
            jax.ShapeDtypeStruct((80, 2 * LANES), F32),
            jax.ShapeDtypeStruct((80, LANES), F32),
        ],
        out_specs=[vmem] * 5,
        scratch_shapes=[
            pltpu.VMEM((240, 4 * elems), BF16),
            pltpu.VMEM((8, 2 * LANES), jnp.int32),
            grid,
        ],
        compiler_params=pltpu.CompilerParams(vmem_limit_bytes=14 << 20),
    )
    earlier = pl.pallas_call(
        functools.partial(early_kernel, hop), in_specs=[vmem] * 6, name="early", **common
    )(*inputs)
    acc, traces, beside, big, own = pl.pallas_call(
        functools.partial(late_kernel, hop), in_specs=[vmem] * 11, name="late", **common
    )(*inputs, *earlier)
    return pl.pallas_call(
        functools.partial(finish_kernel, base, hop, peers),
        out_shape=jax.ShapeDtypeStruct((5, 64, elems), F32),
        in_specs=[vmem] * (peers + 11) + [smem, vmem, vmem],
        out_specs=hbm,
        scratch_shapes=[
            pltpu.VMEM(lanes.shape, F32),
            pltpu.VMEM((6, 80, elems), F32),
            pltpu.VMEM((peers // 2, 240, 2 * slots), BF16),
            pltpu.VMEM((240, 3 * LANES), BF16),
            pltpu.VMEM((4, 80, elems), F32),
            pltpu.VMEM((2, 88, LANES), F32),
            pltpu.VMEM((8, 2 * LANES), jnp.int32),
            grid,
            sems,
        ],
        name="finish",
        compiler_params=pltpu.CompilerParams(vmem_limit_bytes=14 << 20),
    )(
        *arrived,
        acc,
        traces,
        beside,
        big,
        own,
        partner,
        flux_source,
        send_faces,
        mortar_in,
        way,
        level,
        step_size,
        spread,
        gather,
    )


def solution(mesh):
    placed = (
        P(None, None, "dev"),
        P(),
        P("dev"),
        P("dev", None),
        P(None, "dev"),
        P(None, "dev"),
        P("dev"),
        P("dev", None),
        P(None, "dev"),
    )

    return jax.shard_map(
        body, mesh=mesh, in_specs=placed, out_specs=P(None, None, "dev"), check_vma=False
    )
```
